32 devices in a mesh: batch: 4 (over y, x), ctx: 2 (over core), tp: 4 (over z).
Axes of the slice: x: 2, y: 2, z: 4, core: 2. Of those that a mesh axis runs over, the one named last changes fastest.
Arguments:
- hidden_in: bfloat16 [4, 4, 128, 640], P('batch', 'ctx'), may hold values from -6 to 6
- positions: int32 [4, 512], P('batch'), may hold values from 0 to 255, as said below
- block_table: int32 [4], replicated, may hold values from 0 to 3, as said below
- norm_gains: float32 [4, 640], replicated, may hold values from 0.1 to 1.9
- head_norm_gains: float32 [2, 256], replicated, may hold values from 0.6 to 4.5
- query_weight: bfloat16 [640, 1024], P(None, 'tp')
- key_value_weight: bfloat16 [640, 512], replicated
- output_weight: bfloat16 [1024, 640], P('tp'), may hold values from -0.1875 to 0.1875
- gate_weight: bfloat16 [640, 2048], P(None, 'tp'), may hold values from -0.25 to 0.25
- up_weight: bfloat16 [640, 2048], P(None, 'tp'), may hold values from -0.25 to 0.25
- down_weight: bfloat16 [2048, 640], P('tp'), may hold values from -0.125 to 0.125
- out_cotangent: bfloat16 [4, 4, 128, 640], P('batch', 'ctx'), may hold values from -6 to 6
Outputs:
- hidden_out: bfloat16 [4, 4, 128, 640], P('batch', 'ctx')
- input_grad: bfloat16 [4, 4, 128, 640], P('batch', 'ctx')
- query_weight_grad: float32 [640, 1024], P(('batch', 'ctx'), 'tp')
- key_value_weight_grad: float32 [640, 512], P(('batch', 'ctx'))
- output_weight_grad: float32 [1024, 640], P('tp', ('batch', 'ctx'))
- gate_weight_grad: float32 [640, 2048], P(('batch', 'ctx'), 'tp')
- up_weight_grad: float32 [640, 2048], P(('batch', 'ctx'), 'tp')
- down_weight_grad: float32 [2048, 640], P('tp', ('batch', 'ctx'))
- norm_gains_grad: float32 [4, 640], P(None, ('batch', 'ctx'))
- head_norm_gains_grad: float32 [2, 256], P(None, ('batch', 'ctx'))
The draws below stay inside these ranges and needn't reach their ends.
Inputs may be any that keep to these rules, and one draw needn't show every extreme that they name: `positions`: in each sequence the first token has position 0 and every later token has position 0 (a new document begins) or its predecessor's position plus 1; a sequence holds at most 4 documents, and its longest document has exactly 256 tokens. `block_table`: slots 2 k and 2 k + 1 hold two blocks whose numbers add up to 3; every block number appears once.
All inputs are finite; a program needn't handle non-finite values.
Results may differ from the reference program's by a relative error of at most 0.023.
Values may be sent and summed in bfloat16 or wider, within the bound.
No kernel may reach another device: no remote copies, remote signals or barrier semaphores. Data moves between devices by JAX's collectives and lax.ppermute only.
A program may use at most 128 MiB of HBM per device.

```python
import jax
import jax.numpy as jnp
from jax import lax

D = 640
FF = 2048
HEADS = 4
HD = 256
BLK = 128
BLOCKS = 4
SEQ = 512
SEQS = 4


def draw_positions(key, part):
    half = SEQ // 2
    cuts = jnp.sort(jax.random.randint(jax.random.fold_in(key, 1), (SEQS, 2), 1, half), axis=1).astype(jnp.int32)
    place = jax.random.randint(jax.random.fold_in(key, 2), (SEQS,), 0, 4)
    zeros = jnp.zeros((SEQS, 1), jnp.int32)
    ends = jnp.full((SEQS, 1), half, jnp.int32)
    cumulative = jnp.concatenate([zeros, cuts, ends], axis=1)
    pick = (jnp.arange(4, dtype=jnp.int32)[None, :] == place[:, None]).astype(jnp.int32)
    long_start = jnp.sum(cumulative * pick, axis=1)
    moved = jnp.where(cuts <= long_start[:, None], cuts, cuts + half)
    bounds = jnp.concatenate([moved, long_start[:, None], (long_start + half)[:, None]], axis=1)
    index = jnp.arange(SEQ, dtype=jnp.int32)
    starts = jnp.max(jnp.where(bounds[:, :, None] <= index[None, None, :], bounds[:, :, None], 0), axis=1)
    return (index[None, :] - starts).astype(jnp.int32)


def draw_block_table(key, part):
    pairs = BLOCKS // 2
    order = jax.random.permutation(jax.random.fold_in(key, 1), pairs).astype(jnp.int32)
    flips = jax.random.randint(jax.random.fold_in(key, 2), (pairs,), 0, 2)
    first = jnp.where(flips == 1, BLOCKS - 1 - order, order)
    second = BLOCKS - 1 - first
    return jnp.stack([first, second], axis=1).reshape(BLOCKS).astype(jnp.int32)


def draw_head_norm_gains(key, part):
    return jax.random.uniform(key, (2, HD), jnp.float32, 0.6, 1.6)


def draw_query_weight(key, part):
    fresh = jax.random.normal(jax.random.fold_in(key, 12), (D, HEADS * HD), jnp.float32) * D ** (-0.5)
    return fresh.astype(jnp.bfloat16)


def draw_key_value_weight(key, part):
    value_part = jax.random.normal(jax.random.fold_in(key, 13), (D, HD), jnp.float32) * D ** (-0.5)
    key_part = jax.random.normal(jax.random.fold_in(key, 14), (D, HD), jnp.float32) * D ** (-0.5)
    return jnp.concatenate([key_part, value_part], axis=1).astype(jnp.bfloat16)


def level_of(stream_key, dims, shards, low, top_value):
    level = 1.0
    for position, parts in shards:
        steps = jax.random.uniform(jax.random.fold_in(jax.random.fold_in(stream_key, 6), position), (parts,), jnp.float32, low / len(shards), top_value / len(shards))
        level = level * jnp.repeat(jnp.exp(steps), dims[position] // parts).reshape((-1,) + (1,) * (len(dims) - 1 - position))
    return level


def normal_values(rng, extent, spread, limit, split=(), held_as=jnp.bfloat16):
    array = jax.random.normal(rng, extent, jnp.float32) * spread
    if len(split) > 0:
        array = level_of(rng, extent, split, -0.22, 0.18) * array
    return jnp.clip(array, min=-limit, max=limit).astype(held_as)


def setup_inputs(seed: int = 0) -> dict:
    key_list = jax.random.split(jax.random.key(seed), 13)
    return {
        "hidden_in": normal_values(key_list[0], (SEQS, BLOCKS, BLK, D), 1.0, 6.0, ((0, 4), (1, 2))),
        "positions": draw_positions(jax.random.fold_in(key_list[12], 71), 0),
        "block_table": draw_block_table(jax.random.fold_in(key_list[12], 71), 0),
        "norm_gains": jnp.clip(1.0 + 0.18 * jax.random.normal(key_list[3], (4, D), jnp.float32), 0.1, 1.9),
        "head_norm_gains": draw_head_norm_gains(jax.random.fold_in(key_list[12], 71), 0),
        "query_weight": draw_query_weight(jax.random.fold_in(key_list[12], 71), 0),
        "key_value_weight": draw_key_value_weight(jax.random.fold_in(key_list[12], 71), 0),
        "output_weight": normal_values(key_list[7], (HEADS * HD, D), (HEADS * HD) ** -0.5, 0.1875, ((0, 4),)),
        "gate_weight": normal_values(key_list[8], (D, FF), D ** -0.5, 0.25, ((1, 4),)),
        "up_weight": normal_values(key_list[9], (D, FF), D ** -0.5, 0.25, ((1, 4),)),
        "down_weight": normal_values(key_list[10], (FF, D), FF ** -0.5, 0.125, ((0, 4),)),
        "out_cotangent": normal_values(key_list[11], (SEQS, BLOCKS, BLK, D), 1.0, 6.0, ((0, 4), (1, 2))),
    }


epsilon = 1e-06
rope_base = 1000000.0
gelu_coef = 0.7978845608028654

def rms_scale(v):
    return lax.rsqrt(lax.optimization_barrier(jnp.mean(v * v, axis=-1, keepdims=True)) + epsilon)

def rms_back(grad, unit, scale, gain):
    weighted = grad * gain
    return scale * (weighted - unit * lax.optimization_barrier(jnp.mean(unit * weighted, axis=-1, keepdims=True)))

def gelu_slope(v):
    inner = gelu_coef * (v + 0.044715 * v * v * v)
    tanh_val = jnp.tanh(inner)
    return 0.5 * (1.0 + tanh_val) + 0.5 * v * (1.0 - tanh_val * tanh_val) * gelu_coef * (1.0 + 3.0 * 0.044715 * v * v)

def rope_tables(pos_list, width):
    half = width // 2
    freq = rope_base ** (-(jnp.arange(half, dtype=jnp.float32) * 2.0 / width))
    angle = pos_list.astype(jnp.float32)[:, None] * freq[None, :]
    return (jnp.cos(angle), jnp.sin(angle))

def rotate(v, cosine, sine):
    half = v.shape[-1] // 2
    first, second = (v[..., :half], v[..., half:])
    return jnp.concatenate([first * cosine - second * sine, second * cosine + first * sine], axis=-1)

def rotate_back(g, cosine, sine):
    half = g.shape[-1] // 2
    first, second = (g[..., :half], g[..., half:])
    return jnp.concatenate([first * cosine + second * sine, second * cosine - first * sine], axis=-1)

def reference(hidden_in, positions, block_table, norm_gains, head_norm_gains, query_weight, key_value_weight, output_weight, gate_weight, up_weight, down_weight, out_cotangent):
    f32 = jnp.float32
    bf16 = jnp.bfloat16
    inverse = jnp.argsort(block_table).astype(jnp.int32)
    x_nat = jnp.take(hidden_in, inverse, axis=1).reshape(SEQS, SEQ, D)
    cot_nat = jnp.take(out_cotangent, inverse, axis=1).reshape(SEQS, SEQ, D)
    qblock = min(512, SEQ)
    block_count = SEQ // qblock
    starts = jnp.arange(block_count, dtype=jnp.int32) * qblock
    key_index = jnp.arange(SEQ, dtype=jnp.int32)
    root = HD ** (-0.5)

    def allowed_for(start, pos_seq):
        query_index = start + jnp.arange(qblock, dtype=jnp.int32)
        query_pos = lax.dynamic_slice_in_dim(pos_seq, start, qblock)
        return (key_index[None, :] <= query_index[:, None]) & (key_index[None, :] >= (query_index - query_pos)[:, None])

    def sequence_pass(carry, inputs):
        x_seq, cot_seq, pos_seq = inputs
        xs = x_seq.astype(f32)
        scale_in = rms_scale(xs)
        unit_in = xs * scale_in
        normed = (unit_in * norm_gains[0]).astype(bf16)
        query_raw = jnp.dot(normed, query_weight, preferred_element_type=f32).reshape(SEQ, HEADS, HD)
        kv_raw = jnp.dot(normed, key_value_weight, preferred_element_type=f32)
        key_raw = kv_raw[:, :HD]
        value_raw = kv_raw[:, HD:]
        cosine, sine = rope_tables(pos_seq, HD)
        scale_q = rms_scale(query_raw)
        unit_q = query_raw * scale_q
        queries = (rotate(unit_q * head_norm_gains[0], cosine[:, None, :], sine[:, None, :]) * root).astype(bf16)
        scale_k = rms_scale(key_raw)
        unit_k = key_raw * scale_k
        keys = rotate(unit_k * head_norm_gains[1], cosine, sine).astype(bf16)
        values = value_raw.astype(bf16)
        keys32 = keys.astype(f32)
        values32 = values.astype(f32)

        def forward_block(start):
            block_q = lax.dynamic_slice_in_dim(queries, start, qblock).astype(f32)
            allowed = allowed_for(start, pos_seq)
            scores = jnp.einsum('qhd,kd->hqk', block_q, keys32)
            scores = jnp.where(allowed[None], scores, -jnp.inf)
            top = lax.optimization_barrier(jnp.max(scores, axis=2, keepdims=True))
            expo = jnp.exp(scores - top)
            total = lax.optimization_barrier(jnp.sum(expo, axis=2, keepdims=True))
            probs = expo.astype(bf16).astype(f32)
            ctx_block = jnp.einsum('hqk,kd->hqd', probs, values32) / total
            return (jnp.transpose(ctx_block, (1, 0, 2)), top + jnp.log(total))
        ctx_blocks, lse_blocks = lax.map(forward_block, starts)
        context = ctx_blocks.reshape(SEQ, HEADS * HD).astype(bf16)
        attn_out = jnp.dot(context, output_weight, preferred_element_type=f32)
        scale_a = rms_scale(attn_out)
        unit_a = attn_out * scale_a
        mixed = xs + unit_a * norm_gains[1]
        scale_f = rms_scale(mixed)
        unit_f = mixed * scale_f
        ff_in = (unit_f * norm_gains[2]).astype(bf16)
        gate = jnp.dot(ff_in, gate_weight, preferred_element_type=f32)
        up = jnp.dot(ff_in, up_weight, preferred_element_type=f32)
        activated = (jax.nn.gelu(gate, approximate=True) * up).astype(bf16)
        ff_out = jnp.dot(activated, down_weight, preferred_element_type=f32)
        scale_o = rms_scale(ff_out)
        unit_o = ff_out * scale_o
        hidden_out = (mixed + unit_o * norm_gains[3]).astype(bf16)
        cot = cot_seq.astype(f32)
        gain_o = lax.optimization_barrier(jnp.sum(cot * unit_o, axis=0))
        d_ff_out = rms_back(cot, unit_o, scale_o, norm_gains[3]).astype(bf16)
        down_grad = jnp.dot(activated.T, d_ff_out, preferred_element_type=f32)
        d_act = jnp.dot(d_ff_out, down_weight.T, preferred_element_type=f32)
        d_gate = (d_act * up * gelu_slope(gate)).astype(bf16)
        d_up = (d_act * jax.nn.gelu(gate, approximate=True)).astype(bf16)
        gate_grad = jnp.dot(ff_in.T, d_gate, preferred_element_type=f32)
        up_grad = jnp.dot(ff_in.T, d_up, preferred_element_type=f32)
        d_ff_in = jnp.dot(d_gate, gate_weight.T, preferred_element_type=f32) + jnp.dot(d_up, up_weight.T, preferred_element_type=f32)
        gain_f = lax.optimization_barrier(jnp.sum(d_ff_in * unit_f, axis=0))
        d_mixed = cot + rms_back(d_ff_in, unit_f, scale_f, norm_gains[2])
        gain_a = lax.optimization_barrier(jnp.sum(d_mixed * unit_a, axis=0))
        d_attn = rms_back(d_mixed, unit_a, scale_a, norm_gains[1]).astype(bf16)
        out_grad = jnp.dot(context.T, d_attn, preferred_element_type=f32)
        d_context = jnp.dot(d_attn, output_weight.T, preferred_element_type=f32).astype(bf16).reshape(SEQ, HEADS, HD)

        def backward_block(acc, item):
            start, lse = item
            block_q = lax.dynamic_slice_in_dim(queries, start, qblock).astype(f32)
            block_d = lax.dynamic_slice_in_dim(d_context, start, qblock).astype(f32)
            allowed = allowed_for(start, pos_seq)
            scores = jnp.einsum('qhd,kd->hqk', block_q, keys32)
            probs_full = jnp.where(allowed[None], jnp.exp(jnp.where(allowed[None], scores, -jnp.inf) - lse), 0.0)
            d_probs = jnp.einsum('qhd,kd->hqk', block_d, values32)
            delta = lax.optimization_barrier(jnp.sum(probs_full * d_probs, axis=2, keepdims=True))
            d_scores = (probs_full * (d_probs - delta)).astype(bf16).astype(f32)
            d_q = jnp.einsum('hqk,kd->qhd', d_scores, keys32)
            d_k = jnp.einsum('hqk,qhd->kd', d_scores, block_q)
            d_v = jnp.einsum('hqk,qhd->kd', probs_full.astype(bf16).astype(f32), block_d)
            return ((acc[0] + d_k, acc[1] + d_v), d_q)
        zero_kv = jnp.zeros((SEQ, HD), f32)
        (d_keys, d_values), d_q_blocks = lax.scan(backward_block, (zero_kv, zero_kv), (starts, lse_blocks))
        d_queries = d_q_blocks.reshape(SEQ, HEADS, HD)
        d_unit_q = rotate_back(d_queries, cosine[:, None, :], sine[:, None, :]) * root
        gain_q = lax.optimization_barrier(jnp.sum(d_unit_q * unit_q, axis=(0, 1)))
        d_query_raw = rms_back(d_unit_q, unit_q, scale_q, head_norm_gains[0]).astype(bf16).reshape(SEQ, HEADS * HD)
        d_unit_k = rotate_back(d_keys, cosine, sine)
        gain_k = lax.optimization_barrier(jnp.sum(d_unit_k * unit_k, axis=0))
        d_key_raw = rms_back(d_unit_k, unit_k, scale_k, head_norm_gains[1])
        d_kv_raw = jnp.concatenate([d_key_raw, d_values], axis=1).astype(bf16)
        query_grad = jnp.dot(normed.T, d_query_raw, preferred_element_type=f32)
        kv_grad = jnp.dot(normed.T, d_kv_raw, preferred_element_type=f32)
        d_normed = jnp.dot(d_query_raw, query_weight.T, preferred_element_type=f32) + jnp.dot(d_kv_raw, key_value_weight.T, preferred_element_type=f32)
        gain_in = lax.optimization_barrier(jnp.sum(d_normed * unit_in, axis=0))
        input_grad = (d_mixed + rms_back(d_normed, unit_in, scale_in, norm_gains[0])).astype(bf16)
        gains = jnp.stack([gain_in, gain_a, gain_f, gain_o])
        head_gains = jnp.stack([gain_q, gain_k])
        new_carry = (carry[0] + query_grad, carry[1] + kv_grad, carry[2] + out_grad, carry[3] + gate_grad, carry[4] + up_grad, carry[5] + down_grad, carry[6] + gains, carry[7] + head_gains)
        return (new_carry, (hidden_out, input_grad))
    init = (jnp.zeros((D, HEADS * HD), f32), jnp.zeros((D, 2 * HD), f32), jnp.zeros((HEADS * HD, D), f32), jnp.zeros((D, FF), f32), jnp.zeros((D, FF), f32), jnp.zeros((FF, D), f32), jnp.zeros((4, D), f32), jnp.zeros((2, HD), f32))
    grads, (outs_nat, dx_nat) = lax.scan(sequence_pass, init, (x_nat, cot_nat, positions))
    hidden_out = jnp.take(outs_nat.reshape(SEQS, BLOCKS, BLK, D), block_table, axis=1)
    input_grad = jnp.take(dx_nat.reshape(SEQS, BLOCKS, BLK, D), block_table, axis=1)
    return (hidden_out, input_grad, grads[0], grads[1], grads[2], grads[3], grads[4], grads[5], grads[6], grads[7])
```

```python
import functools

import jax
import jax.numpy as jnp
from jax import lax
from jax.experimental import pallas as pl
from jax.experimental.pallas import tpu as pltpu
from jax.sharding import PartitionSpec as P


epsilon = 1e-06
rope_base = 1000000.0
gelu_coef = 0.7978845608028654
f32 = jnp.float32
bf16 = jnp.bfloat16


def rms_scale(v):
    return lax.rsqrt(jnp.mean(v * v, axis=-1, keepdims=True) + epsilon)


def rms_back(grad, unit, scale, gain):
    weighted = grad * gain
    return scale * (weighted - unit * jnp.mean(unit * weighted, axis=-1, keepdims=True))


def rotate(v, cosine, sine):
    half = v.shape[-1] // 2
    first, second = (v[..., :half], v[..., half:])
    return jnp.concatenate(
        [first * cosine - second * sine, second * cosine + first * sine], axis=-1
    )


def rotate_back(g, cosine, sine):
    half = g.shape[-1] // 2
    first, second = (g[..., :half], g[..., half:])
    return jnp.concatenate(
        [first * cosine + second * sine, second * cosine - first * sine], axis=-1
    )


def product(left, right):
    return jnp.dot(left, right, preferred_element_type=f32)


def lead_product(left, right):
    return lax.dot_general(left, right, (((0,), (0,)), ((), ())), preferred_element_type=f32)


def back_product(left, right):
    return lax.dot_general(left, right, (((1,), (1,)), ((), ())), preferred_element_type=f32)


def kernel_call(name, body, args, outs, scratch=(), tables=0, flops=0):
    moved = sum(a.size * a.dtype.itemsize for a in args)
    moved += sum(functools.reduce(lambda m, n: m * n, s, 1) * jnp.dtype(d).itemsize for s, d in outs)
    work = sum(functools.reduce(lambda m, n: m * n, s.shape, 1) * jnp.dtype(s.dtype).itemsize for s in scratch)
    limit = min(60 << 20, (8 << 20) + 2 * (moved + work))
    return pl.pallas_call(
        body,
        out_shape=[jax.ShapeDtypeStruct(s, d) for s, d in outs],
        in_specs=[pl.BlockSpec(memory_space=pltpu.SMEM)] * tables
        + [pl.BlockSpec(memory_space=pltpu.VMEM)] * (len(args) - tables),
        out_specs=[pl.BlockSpec(memory_space=pltpu.VMEM)] * len(outs),
        scratch_shapes=list(scratch),
        name=name,
        cost_estimate=pl.CostEstimate(flops=flops, bytes_accessed=moved, transcendentals=0),
        compiler_params=pltpu.CompilerParams(vmem_limit_bytes=limit),
    )(*args)


def swap(x, axis, size, k):
    return lax.ppermute(x, axis, [(i, i ^ k) for i in range(size)])


def on_device(
    hidden_in,
    positions,
    block_table,
    norm_gains,
    head_norm_gains,
    query_weight,
    key_value_weight,
    output_weight,
    gate_weight,
    up_weight,
    down_weight,
    out_cotangent,
):
    n_tp = lax.axis_size("tp")
    n_ctx = lax.axis_size("ctx")
    n_batch = lax.axis_size("batch")
    blocks, block_len, width = hidden_in.shape[1:]
    rows = blocks * block_len
    head_dim = key_value_weight.shape[1] // 2
    half = head_dim // 2
    heads = query_weight.shape[1] // head_dim
    q_width = heads * head_dim
    ff = gate_weight.shape[1]
    seq = positions.shape[1]
    root = head_dim ** (-0.5)
    share = rows // n_tp
    shards = n_batch * n_ctx
    out_rows = width // shards
    head_rows = head_dim // shards
    paired = n_ctx == 2 and n_batch in (2, 4)

    hidden = hidden_in.reshape(rows, width)
    cot = out_cotangent.reshape(rows, width)
    freq = (rope_base ** (-(jnp.arange(half, dtype=f32) * 2.0 / head_dim))).reshape(1, half)

    def part(k):
        return slice(k * share, (k + 1) * share)

    def own_rows(k):
        return pl.ds(pl.multiple_of((lax.axis_index("tp") ^ k) * share, share), share)

    def store_parts(value, refs):
        for k in range(n_tp):
            refs[k][...] = value[part(k)].astype(refs[k].dtype)

    part_outs = [((share, width), f32)] + [((share, width), bf16)] * (n_tp - 1)

    def scatter(parts):
        return [parts[0]] + [swap(parts[k], "tp", n_tp, k) for k in range(1, n_tp)]

    def gather(x):
        return [x] + [swap(x, "tp", n_tp, k) for k in range(1, n_tp)]

    def joined(refs):
        return jnp.concatenate([r[...] for r in refs], axis=0)

    def summed(refs):
        total = refs[0][...].astype(f32)
        for r in refs[1:]:
            total = total + r[...].astype(f32)
        return total

    def pre_body(table, hid, pos, gains, hgains, freqs, wkv, normed_o, kv_o, unit_o, scale_o, cos_o, sin_o, idx_o, start_o, col_pos, col_idx):
        eye = lax.broadcasted_iota(jnp.int32, (block_len, block_len), 0) == lax.broadcasted_iota(
            jnp.int32, (block_len, block_len), 1
        )
        for j in range(blocks):
            t = table[lax.axis_index("ctx") * blocks + j]
            line = pos[:, pl.ds(pl.multiple_of(t * block_len, block_len), block_len)].astype(f32)
            column = jnp.sum(jnp.where(eye, line, 0.0), axis=1, keepdims=True)
            place = lax.broadcasted_iota(jnp.int32, (block_len, 1), 0) + t * block_len
            col_pos[j * block_len : (j + 1) * block_len, :] = column
            col_idx[j * block_len : (j + 1) * block_len, :] = place.astype(f32)
        for k in range(n_tp):
            at = own_rows(k)
            x = hid[at, :].astype(f32)
            normed_o[part(k), :] = (x * rms_scale(x) * gains[0:1, :]).astype(bf16)
            p = col_pos[at, :]
            angle = p * freqs[...]
            cos_o[part(k), :] = jnp.cos(angle)
            sin_o[part(k), :] = jnp.sin(angle)
            idx_o[part(k), :] = col_idx[at, :]
            start_o[part(k), :] = col_idx[at, :] - p
        kv = product(normed_o[...], wkv[...])
        key = kv[:, :head_dim]
        scale = rms_scale(key)
        unit = key * scale
        unit_o[...] = unit
        scale_o[...] = scale
        kv_o[:, :head_dim] = rotate(unit * hgains[1:2, :], cos_o[...], sin_o[...]).astype(bf16)
        kv_o[:, head_dim:] = kv[:, head_dim:].astype(bf16)

    normed, kv_mine, unit_k, scale_k, cosine, sine, idx, start = kernel_call(
        "pre",
        pre_body,
        (block_table, hidden, positions, norm_gains, head_norm_gains, freq, key_value_weight),
        [
            ((rows, width), bf16),
            ((rows, 2 * head_dim), bf16),
            ((rows, head_dim), f32),
            ((rows, 1), f32),
            ((rows, half), f32),
            ((rows, half), f32),
            ((rows, 1), f32),
            ((rows, 1), f32),
        ],
        scratch=[pltpu.VMEM((rows, 1), f32), pltpu.VMEM((rows, 1), f32)],
        tables=1,
    )

    if paired:
        kvs = [kv_mine, swap(kv_mine, "ctx", n_ctx, 1)]
    else:
        kvs = [lax.all_gather(kv_mine, "ctx", axis=0, tiled=True)]

    def query_body(nrm, wq, hgains, cos, sin, q_o, unit_o, scale_o):
        raw = product(nrm[...], wq[...])
        for h in range(heads):
            cols = slice(h * head_dim, (h + 1) * head_dim)
            scale = rms_scale(raw[:, cols])
            unit = raw[:, cols] * scale
            unit_o[:, cols] = unit
            scale_o[:, h : h + 1] = scale
            q_o[:, cols] = (rotate(unit * hgains[0:1, :], cos[...], sin[...]) * root).astype(bf16)

    queries, unit_q, scale_q = kernel_call(
        "query",
        query_body,
        (normed, query_weight, head_norm_gains, cosine, sine),
        [((rows, q_width), bf16), ((rows, q_width), f32), ((rows, heads), f32)],
    )

    def attend_body(*refs):
        table, q, idx_r, start_r, wo = refs[:5]
        kv = refs[5 : 5 + len(kvs)]
        probs_o, context_o = refs[5 + len(kvs) : 7 + len(kvs)]
        outs = refs[7 + len(kvs) :]
        tp = lax.axis_index("tp")
        ctx = lax.axis_index("ctx")
        order = [ctx, ctx ^ 1] if paired else list(range(n_ctx))
        lane = lax.broadcasted_iota(jnp.int32, (1, seq), 1)
        key_idx = lane
        for m, rank in enumerate(order):
            for k in range(n_tp):
                first = (tp ^ k) * share
                base = table[rank * blocks + lax.div(first, block_len)] * block_len
                base = base + lax.rem(first, block_len)
                seg = m * n_tp + k
                key_idx = jnp.where(
                    (lane >= seg * share) & (lane < (seg + 1) * share), lane + (base - seg * share), key_idx
                )
        key_idx = key_idx.astype(f32)
        allowed = (key_idx <= idx_r[...]) & (key_idx >= start_r[...])
        for h in range(heads):
            cols = slice(h * head_dim, (h + 1) * head_dim)
            scores = jnp.concatenate(
                [back_product(q[:, cols], r[:, :head_dim]) for r in kv], axis=1
            )
            scores = jnp.where(allowed, scores, -jnp.inf)
            top = jnp.max(scores, axis=1, keepdims=True)
            expo = jnp.exp(scores - top)
            inverse = 1.0 / jnp.sum(expo, axis=1, keepdims=True)
            probs_o[h] = expo * inverse
            probs = expo.astype(bf16)
            length = seq // len(kvs)
            mixed = product(probs[:, :length], kv[0][:, head_dim:])
            for m in range(1, len(kvs)):
                mixed = mixed + product(probs[:, m * length : (m + 1) * length], kv[m][:, head_dim:])
            context_o[:, cols] = (mixed * inverse).astype(bf16)
        store_parts(product(context_o[...], wo[...]), outs)

    attended = kernel_call(
        "attend",
        attend_body,
        (block_table, queries, idx, start, output_weight, *kvs),
        [((heads, rows, seq), f32), ((rows, q_width), bf16)] + part_outs,
        tables=1,
    )
    probs, context = attended[:2]
    attn_parts = scatter(attended[2:])

    def mix_body(hid, gains, *refs):
        attn = summed(refs[:n_tp])
        unit_o, scale_o, mixed_o, ffin_o = refs[n_tp:]
        scale = rms_scale(attn)
        unit = attn * scale
        mixed = hid[own_rows(0), :].astype(f32) + unit * gains[1:2, :]
        unit_o[...] = unit
        scale_o[...] = scale
        mixed_o[...] = mixed
        ffin_o[...] = (mixed * rms_scale(mixed) * gains[2:3, :]).astype(bf16)

    unit_a, scale_a, mixed, ff_mine = kernel_call(
        "mix",
        mix_body,
        (hidden, norm_gains, *attn_parts),
        [((share, width), f32), ((share, 1), f32), ((share, width), f32), ((share, width), bf16)],
    )
    ff_in = gather(ff_mine)

    def ff_body(wg, wu, wd, *refs):
        x = joined(refs[:n_tp])
        gate_o, up_o, act_o = refs[n_tp : n_tp + 3]
        gate = product(x, wg[...])
        up = product(x, wu[...])
        gate_o[...] = gate
        up_o[...] = up
        act = 0.5 * gate * (1.0 + jnp.tanh(gelu_coef * (gate + 0.044715 * gate * gate * gate))) * up
        act_o[...] = act.astype(bf16)
        store_parts(product(act_o[...], wd[...]), refs[n_tp + 3 :])

    fed = kernel_call(
        "feed",
        ff_body,
        (gate_weight, up_weight, down_weight, *ff_in),
        [((rows, ff), f32), ((rows, ff), f32), ((rows, ff), bf16)] + part_outs,
    )
    gate, up, activated = fed[:3]
    ff_parts = scatter(fed[3:])

    def slope_body(gate_r, up_r, gelu_o, slope_o):
        v = gate_r[...]
        inner = gelu_coef * (v + 0.044715 * v * v * v)
        tanh_val = jnp.tanh(inner)
        gelu_o[...] = 0.5 * v * (1.0 + tanh_val)
        slope = 0.5 * (1.0 + tanh_val) + 0.5 * v * (1.0 - tanh_val * tanh_val) * gelu_coef * (
            1.0 + 3.0 * 0.044715 * v * v
        )
        slope_o[...] = slope * up_r[...]

    gelu, up_slope = kernel_call(
        "slope", slope_body, (gate, up), [((rows, ff), f32), ((rows, ff), f32)]
    )

    def out_body(gains, mixed_r, cot_r, *refs):
        ff_out = summed(refs[:n_tp])
        hidden_o, dff_o, gain_o = refs[n_tp:]
        scale = rms_scale(ff_out)
        unit = ff_out * scale
        hidden_o[...] = (mixed_r[...] + unit * gains[3:4, :]).astype(bf16)
        grad = cot_r[own_rows(0), :].astype(f32)
        gain_o[...] = jnp.sum(grad * unit, axis=0, keepdims=True)
        dff_o[...] = rms_back(grad, unit, scale, gains[3:4, :]).astype(bf16)

    hidden_mine, dff_mine, gain_o = kernel_call(
        "turn",
        out_body,
        (norm_gains, mixed, cot, *ff_parts),
        [((share, width), bf16), ((share, width), bf16), ((1, width), f32)],
    )
    d_ff = gather(dff_mine)

    def ff_back_body(wg, wu, wd, gelu_r, slope_r, *refs):
        d_out = joined(refs[:n_tp])
        dgate_o, dup_o = refs[n_tp : n_tp + 2]
        d_act = back_product(d_out, wd[...])
        dgate_o[...] = (d_act * slope_r[...]).astype(bf16)
        dup_o[...] = (d_act * gelu_r[...]).astype(bf16)
        store_parts(back_product(dgate_o[...], wg[...]) + back_product(dup_o[...], wu[...]), refs[n_tp + 2 :])

    backed = kernel_call(
        "feed_back",
        ff_back_body,
        (gate_weight, up_weight, down_weight, gelu, up_slope, *d_ff),
        [((rows, ff), bf16), ((rows, ff), bf16)] + part_outs,
    )
    d_gate, d_up = backed[:2]
    dffin_parts = scatter(backed[2:])

    def arrange(acc, outs):
        if not paired:
            outs[0][...] = acc[...]
            return
        batch = lax.axis_index("batch")
        ctx = lax.axis_index("ctx")
        for side in range(2):
            for k in range(n_batch):
                first = ((batch ^ k) * n_ctx + (ctx ^ side)) * out_rows
                outs[side][k * out_rows : (k + 1) * out_rows, :] = acc[
                    pl.ds(pl.multiple_of(first, out_rows), out_rows), :
                ].astype(bf16)

    def grad_call(name, body, args, columns):
        if paired:
            outs = [((n_batch * out_rows, columns), bf16)] * 2
        else:
            outs = [((width, columns), f32)]
        return kernel_call(name, body, args, outs, scratch=[pltpu.VMEM((width, columns), f32)])

    def reduce_grads(name, grads):
        if not paired:
            return lax.psum_scatter(grads[0], ("batch", "ctx"), scatter_dimension=0, tiled=True)
        keep, send = grads
        columns = keep.shape[1]
        got = swap(send, "ctx", n_ctx, 1)

        def add_body(a, b, *outs):
            total = a[...].astype(f32) + b[...].astype(f32)
            for k in range(n_batch):
                outs[k][...] = total[k * out_rows : (k + 1) * out_rows].astype(outs[k].dtype)

        parts = kernel_call(
            name,
            add_body,
            (keep, got),
            [((out_rows, columns), f32)] + [((out_rows, columns), bf16)] * (n_batch - 1),
        )
        total = parts[0]
        for k in range(1, n_batch):
            total = total + swap(parts[k], "batch", n_batch, k).astype(f32)
        return total

    def ff_grad_body(act, dgate, dup, *refs):
        x = joined(refs[:n_tp])
        d_out = joined(refs[n_tp : 2 * n_tp])
        acc = refs[-1]
        acc[:, :ff] = lead_product(x, dgate[...])
        acc[:, ff : 2 * ff] = lead_product(x, dup[...])
        acc[:, 2 * ff :] = lead_product(d_out, act[...])
        arrange(acc, refs[2 * n_tp : -1])

    ff_grads = reduce_grads(
        "feed_add", grad_call("feed_grad", ff_grad_body, (activated, d_gate, d_up, *ff_in, *d_ff), 3 * ff)
    )

    def mix_back_body(gains, mixed_r, unit_r, scale_r, cot_r, *refs):
        d_in = summed(refs[:n_tp])
        dmixed_o, dattn_o, gain_f_o, gain_a_o = refs[n_tp:]
        mixed_v = mixed_r[...]
        scale = rms_scale(mixed_v)
        unit_f = mixed_v * scale
        gain_f_o[...] = jnp.sum(d_in * unit_f, axis=0, keepdims=True)
        d_mix = cot_r[own_rows(0), :].astype(f32) + rms_back(d_in, unit_f, scale, gains[2:3, :])
        dmixed_o[...] = d_mix
        unit = unit_r[...]
        gain_a_o[...] = jnp.sum(d_mix * unit, axis=0, keepdims=True)
        dattn_o[...] = rms_back(d_mix, unit, scale_r[...], gains[1:2, :]).astype(bf16)

    d_mixed, dattn_mine, gain_f, gain_a = kernel_call(
        "mix_back",
        mix_back_body,
        (norm_gains, mixed, unit_a, scale_a, cot, *dffin_parts),
        [((share, width), f32), ((share, width), bf16), ((1, width), f32), ((1, width), f32)],
    )
    d_attn = gather(dattn_mine)

    def attend_back_body(*refs):
        wo, probs_r, q = refs[:3]
        kv = refs[3 : 3 + len(kvs)]
        d_out = joined(refs[3 + len(kvs) : 3 + len(kvs) + n_tp])
        dq_o = refs[3 + len(kvs) + n_tp]
        dkv_o = refs[4 + len(kvs) + n_tp :]
        d_context = back_product(d_out, wo[...]).astype(bf16)
        length = seq // len(kvs)
        for h in range(heads):
            cols = slice(h * head_dim, (h + 1) * head_dim)
            probs_v = probs_r[h]
            d_probs = jnp.concatenate(
                [back_product(d_context[:, cols], r[:, head_dim:]) for r in kv], axis=1
            )
            delta = jnp.sum(probs_v * d_probs, axis=1, keepdims=True)
            d_scores = (probs_v * (d_probs - delta)).astype(bf16)
            rounded = probs_v.astype(bf16)
            d_q = None
            for m, r in enumerate(kv):
                span = slice(m * length, (m + 1) * length)
                term = product(d_scores[:, span], r[:, :head_dim])
                d_q = term if d_q is None else d_q + term
                d_k = lead_product(d_scores[:, span], q[:, cols])
                d_v = lead_product(rounded[:, span], d_context[:, cols])
                if h > 0:
                    d_k = d_k + dkv_o[m][:, :head_dim].astype(f32)
                    d_v = d_v + dkv_o[m][:, head_dim:].astype(f32)
                dkv_o[m][:, :head_dim] = d_k.astype(dkv_o[m].dtype)
                dkv_o[m][:, head_dim:] = d_v.astype(dkv_o[m].dtype)
            dq_o[:, cols] = d_q

    if paired:
        dkv_outs = [((rows, 2 * head_dim), f32), ((rows, 2 * head_dim), f32 if heads > 1 else bf16)]
    else:
        dkv_outs = [((seq, 2 * head_dim), f32)]
    attended_back = kernel_call(
        "attend_back",
        attend_back_body,
        (output_weight, probs, queries, *kvs, *d_attn),
        [((rows, q_width), f32)] + dkv_outs,
    )
    d_q = attended_back[0]
    if paired:
        dkv_terms = [attended_back[1], swap(attended_back[2], "ctx", n_ctx, 1)]
    else:
        dkv_terms = [lax.psum_scatter(attended_back[1], "ctx", scatter_dimension=0, tiled=True)]

    hidden_mine, *_ = lax.optimization_barrier((hidden_mine, *d_attn))
    hidden_parts = gather(hidden_mine)

    def query_back_body(dq, unit_r, scale_r, cos, sin, hgains, wq, draw_o, dn_o, gain_o):
        gain = jnp.zeros((1, head_dim), f32)
        for h in range(heads):
            cols = slice(h * head_dim, (h + 1) * head_dim)
            d_unit = rotate_back(dq[:, cols], cos[...], sin[...]) * root
            unit = unit_r[:, cols]
            gain = gain + jnp.sum(d_unit * unit, axis=0, keepdims=True)
            draw_o[:, cols] = rms_back(d_unit, unit, scale_r[:, h : h + 1], hgains[0:1, :]).astype(bf16)
        gain_o[...] = gain
        dn_o[...] = back_product(draw_o[...], wq[...])

    d_query_raw, dn_query, gain_q = kernel_call(
        "query_back",
        query_back_body,
        (d_q, unit_q, scale_q, cosine, sine, head_norm_gains, query_weight),
        [((rows, q_width), bf16), ((rows, width), f32), ((1, head_dim), f32)],
    )

    def out_grad_body(ctx_r, *refs):
        acc = refs[-1]
        acc[...] = lead_product(joined(refs[:n_tp]), ctx_r[...])
        arrange(acc, refs[n_tp:-1])

    out_grads = reduce_grads("out_add", grad_call("out_grad", out_grad_body, (context, *d_attn), q_width))

    def pre_back_body(dn, unit_r, scale_r, cos, sin, hgains, wkv, *refs):
        count = len(dkv_terms)
        d_kv = summed(refs[:count])
        draw_o, gain_o = refs[count : count + 2]
        d_unit = rotate_back(d_kv[:, :head_dim], cos[...], sin[...])
        unit = unit_r[...]
        gain_o[...] = jnp.sum(d_unit * unit, axis=0, keepdims=True)
        draw_o[:, :head_dim] = rms_back(d_unit, unit, scale_r[...], hgains[1:2, :]).astype(bf16)
        draw_o[:, head_dim:] = d_kv[:, head_dim:].astype(bf16)
        store_parts(dn[...] + back_product(draw_o[...], wkv[...]), refs[count + 2 :])

    pre_backed = kernel_call(
        "pre_back",
        pre_back_body,
        (dn_query, unit_k, scale_k, cosine, sine, head_norm_gains, key_value_weight, *dkv_terms),
        [((rows, 2 * head_dim), bf16), ((1, head_dim), f32)] + part_outs,
    )
    d_kv_raw, gain_k = pre_backed[:2]
    dn_terms = pre_backed[2:]
    dn_parts = scatter(dn_terms)

    lanes = 128
    kv_at = q_width
    gain_at = q_width + 2 * head_dim

    def last_grad_body(nrm, draw, dkv, hid, g_o, g_f, g_a, g_q, g_k, *refs):
        acc = refs[-1]
        acc[:, :kv_at] = lead_product(nrm[...], draw[...])
        acc[:, kv_at:gain_at] = lead_product(nrm[...], dkv[...])
        g_in = jnp.zeros((1, width), f32)
        for k in range(n_tp):
            x = hid[own_rows(k), :].astype(f32)
            g_in = g_in + jnp.sum(refs[k][...].astype(f32) * x * rms_scale(x), axis=0, keepdims=True)
        line = lax.broadcasted_iota(jnp.int32, (lanes, width), 0)
        packed = jnp.where(line == 0, g_in, 0.0)
        for at, row in enumerate((g_a, g_f, g_o), 1):
            packed = jnp.where(line == at, row[...], packed)
        acc[:, gain_at:] = packed.T
        line = lax.broadcasted_iota(jnp.int32, (lanes, head_dim), 0)
        packed = jnp.where(line == 4, g_q[...], jnp.where(line == 5, g_k[...], 0.0)).T
        for d in range(shards):
            at = slice(d * out_rows, d * out_rows + head_rows)
            acc[at, gain_at:] = acc[at, gain_at:] + packed[d * head_rows : (d + 1) * head_rows]
        arrange(acc, refs[n_tp:-1])

    last_grads = reduce_grads(
        "last_add",
        grad_call(
            "last_grad",
            last_grad_body,
            (normed, d_query_raw, d_kv_raw, hidden, gain_o, gain_f, gain_a, gain_q, gain_k, *dn_terms),
            gain_at + lanes,
        ),
    )
    own_kv = last_grads[:, kv_at:].astype(bf16)
    kv_total = last_grads[:, kv_at:]
    for k in range(1, n_tp):
        kv_total = kv_total + swap(own_kv, "tp", n_tp, k).astype(f32)

    def input_back_body(hid, gains, dmix, *refs):
        d_normed = summed(refs[:n_tp])
        x = hid[own_rows(0), :].astype(f32)
        scale = rms_scale(x)
        refs[n_tp][...] = (dmix[...] + rms_back(d_normed, x * scale, scale, gains[0:1, :])).astype(bf16)

    (input_mine,) = kernel_call(
        "input_back", input_back_body, (hidden, norm_gains, d_mixed, *dn_parts), [((share, width), bf16)]
    )
    input_parts = gather(input_mine)

    def place_body(*refs):
        for k in range(n_tp):
            refs[n_tp][own_rows(k), :] = refs[k][...]

    def placed(name, parts):
        (whole,) = kernel_call(name, place_body, tuple(parts), [((rows, width), bf16)])
        return whole.reshape(hidden_in.shape)

    return (
        placed("place_hidden", hidden_parts),
        placed("place_grad", input_parts),
        last_grads[:, :kv_at],
        kv_total[:, : 2 * head_dim],
        out_grads.T,
        ff_grads[:, :ff],
        ff_grads[:, ff : 2 * ff],
        ff_grads[:, 2 * ff :].T,
        kv_total[:, 2 * head_dim : 2 * head_dim + 4].T,
        kv_total[:head_rows, 2 * head_dim + 4 : 2 * head_dim + 6].T,
    )


def solution(mesh):
    return jax.shard_map(
        on_device,
        mesh=mesh,
        in_specs=(
            P("batch", "ctx", None, None),
            P("batch", None),
            P(),
            P(),
            P(),
            P(None, "tp"),
            P(),
            P("tp", None),
            P(None, "tp"),
            P(None, "tp"),
            P("tp", None),
            P("batch", "ctx", None, None),
        ),
        out_specs=(
            P("batch", "ctx", None, None),
            P("batch", "ctx", None, None),
            P(("batch", "ctx"), "tp"),
            P(("batch", "ctx"), None),
            P("tp", ("batch", "ctx")),
            P(("batch", "ctx"), "tp"),
            P(("batch", "ctx"), "tp"),
            P("tp", ("batch", "ctx")),
            P(None, ("batch", "ctx")),
            P(None, ("batch", "ctx")),
        ),
        check_vma=False,
    )
```

```python
import functools

import jax
import jax.numpy as jnp
from jax import lax
from jax.experimental import pallas as pl
from jax.experimental.pallas import tpu as pltpu
from jax.sharding import PartitionSpec as P


epsilon = 1e-06
rope_base = 1000000.0
gelu_coef = 0.7978845608028654
f32 = jnp.float32
bf16 = jnp.bfloat16


def rms_scale(v):
    return lax.rsqrt(jnp.mean(v * v, axis=-1, keepdims=True) + epsilon)


def rms_back(grad, unit, scale, gain):
    weighted = grad * gain
    return scale * (weighted - unit * jnp.mean(unit * weighted, axis=-1, keepdims=True))


def rotate(v, cosine, sine):
    half = v.shape[-1] // 2
    first, second = (v[..., :half], v[..., half:])
    return jnp.concatenate(
        [first * cosine - second * sine, second * cosine + first * sine], axis=-1
    )


def rotate_back(g, cosine, sine):
    half = g.shape[-1] // 2
    first, second = (g[..., :half], g[..., half:])
    return jnp.concatenate(
        [first * cosine + second * sine, second * cosine - first * sine], axis=-1
    )


def product(left, right):
    return jnp.dot(left, right, preferred_element_type=f32)


def lead_product(left, right):
    return lax.dot_general(left, right, (((0,), (0,)), ((), ())), preferred_element_type=f32)


def back_product(left, right):
    return lax.dot_general(left, right, (((1,), (1,)), ((), ())), preferred_element_type=f32)


def kernel_call(body, args, outs, scratch=(), tables=0, flops=0):
    moved = sum(a.size * a.dtype.itemsize for a in args)
    moved += sum(functools.reduce(lambda m, n: m * n, s, 1) * jnp.dtype(d).itemsize for s, d in outs)
    work = sum(functools.reduce(lambda m, n: m * n, s.shape, 1) * jnp.dtype(s.dtype).itemsize for s in scratch)
    limit = min(60 << 20, (8 << 20) + 2 * (moved + work))
    return pl.pallas_call(
        body,
        out_shape=[jax.ShapeDtypeStruct(s, d) for s, d in outs],
        in_specs=[pl.BlockSpec(memory_space=pltpu.SMEM)] * tables
        + [pl.BlockSpec(memory_space=pltpu.VMEM)] * (len(args) - tables),
        out_specs=[pl.BlockSpec(memory_space=pltpu.VMEM)] * len(outs),
        scratch_shapes=list(scratch),
        cost_estimate=pl.CostEstimate(flops=flops, bytes_accessed=moved, transcendentals=0),
        compiler_params=pltpu.CompilerParams(vmem_limit_bytes=limit),
    )(*args)


def swap(x, axis, size, k):
    return lax.ppermute(x, axis, [(i, i ^ k) for i in range(size)])


def after(x, *others):
    return lax.optimization_barrier((x, *others))[0]


def on_device(
    hidden_in,
    positions,
    block_table,
    norm_gains,
    head_norm_gains,
    query_weight,
    key_value_weight,
    output_weight,
    gate_weight,
    up_weight,
    down_weight,
    out_cotangent,
):
    n_tp = lax.axis_size("tp")
    n_ctx = lax.axis_size("ctx")
    n_batch = lax.axis_size("batch")
    blocks, block_len, width = hidden_in.shape[1:]
    rows = blocks * block_len
    head_dim = key_value_weight.shape[1] // 2
    half = head_dim // 2
    heads = query_weight.shape[1] // head_dim
    q_width = heads * head_dim
    ff = gate_weight.shape[1]
    seq = positions.shape[1]
    root = head_dim ** (-0.5)
    share = rows // 2
    unit_len = min(share, block_len)
    peers = tuple(range(2, n_tp, 2))
    copies = n_tp // 2
    shards = n_batch * n_ctx
    out_rows = width // shards
    head_rows = head_dim // shards
    paired = n_ctx == 2 and n_batch in (2, 4)

    hidden = hidden_in.reshape(rows, width)
    cot = out_cotangent.reshape(rows, width)
    freq = (rope_base ** (-(jnp.arange(half, dtype=f32) * 2.0 / head_dim))).reshape(1, half)

    def part(k):
        return slice(k * share, (k + 1) * share)

    def own_rows(k):
        return pl.ds(pl.multiple_of(((lax.axis_index("tp") & 1) ^ k) * share, share), share)

    def neighbour(x):
        return swap(x, "tp", n_tp, 1)

    def other_core(x):
        return swap(x, "ctx", n_ctx, 1)

    def exchanged(x):
        return [x] + [swap(x, "tp", n_tp, k) for k in peers]

    def joined(refs, columns=slice(None)):
        return jnp.concatenate([r[:, columns] for r in refs], axis=0)

    def summed(refs):
        total = refs[0][...].astype(f32)
        for r in refs[1:]:
            total = total + r[...].astype(f32)
        return total

    def own_half(length):
        half_length = length // 2
        return pl.ds(pl.multiple_of((lax.axis_index("ctx") & 1) * half_length, half_length), half_length)

    def own_piece(length):
        piece = length // (2 * n_batch)
        place = ((lax.axis_index("ctx") & 1) * n_batch + lax.axis_index("batch")) * piece
        return pl.ds(pl.multiple_of(place, piece), piece)

    up_piece = width // (2 * n_batch)
    down_piece = ff // (2 * n_batch)
    piece_rows = max(up_piece, down_piece)

    def pack_body(gate, up, down, gate_o, piece_o, sem):
        if up_piece < piece_rows:
            piece_o[up_piece:, :ff] = jnp.zeros((piece_rows - up_piece, ff), bf16)
        if down_piece < piece_rows:
            piece_o[down_piece:, ff:] = jnp.zeros((piece_rows - down_piece, width), bf16)
        moves = [
            pltpu.make_async_copy(up.at[own_piece(width), :], piece_o.at[:up_piece, :ff], sem.at[0]),
            pltpu.make_async_copy(down.at[own_piece(ff), :], piece_o.at[:down_piece, ff:], sem.at[1]),
            pltpu.make_async_copy(gate.at[own_half(width), :], gate_o, sem.at[2]),
        ]
        for move in moves:
            move.start()
        for move in moves:
            move.wait()

    gate_pack, piece_pack = pl.pallas_call(
        pack_body,
        out_shape=[jax.ShapeDtypeStruct((width // 2, ff), bf16), jax.ShapeDtypeStruct((piece_rows, ff + width), bf16)],
        in_specs=[pl.BlockSpec(memory_space=pltpu.HBM)] * 3,
        out_specs=[pl.BlockSpec(memory_space=pltpu.VMEM)] * 2,
        scratch_shapes=[pltpu.SemaphoreType.DMA((3,))],
        name="pack",
        compiler_params=pltpu.CompilerParams(vmem_limit_bytes=16 << 20),
    )(*(pltpu.with_memory_space_constraint(w, pltpu.HBM) for w in (gate_weight, up_weight, down_weight)))
    gate_near = neighbour(gate_pack)
    piece_near = neighbour(piece_pack)
    pieces = [piece_near] + [swap(piece_near, "batch", n_batch, k) for k in range(1, n_batch)]

    def stack_body(*refs):
        up_o, down_o = refs[n_batch:]
        for k in range(n_batch):
            b = lax.axis_index("batch") ^ k
            up_o[pl.ds(pl.multiple_of(b * up_piece, up_piece), up_piece), :] = refs[k][:up_piece, :ff]
            down_o[pl.ds(pl.multiple_of(b * down_piece, down_piece), down_piece), :] = refs[k][
                :down_piece, ff:
            ]

    up_near, down_near = kernel_call(stack_body, tuple(pieces), [((width // 2, ff), bf16), ((ff // 2, width), bf16)])

    def whole_body(*refs):
        for mine, far, whole in zip(refs[:3], refs[3:6], refs[6:]):
            length = mine.shape[0]
            for k, ref in enumerate((mine, far)):
                place = ((lax.axis_index("ctx") & 1) ^ k) * length
                whole[pl.ds(pl.multiple_of(place, length), length), :] = ref[...]

    halves = (gate_near, up_near, down_near)
    near_weights = kernel_call(
        whole_body,
        halves + tuple(other_core(h) for h in halves),
        [((width, ff), bf16), ((width, ff), bf16), ((ff, width), bf16)],
    )

    def pre_body(table, hid, pos, gains, hgains, freqs, wkv, normed_o, kv_o, unit_o, scale_o, cos_o, sin_o, idx_o, start_o, col_pos, col_idx):
        eye = lax.broadcasted_iota(jnp.int32, (block_len, block_len), 0) == lax.broadcasted_iota(
            jnp.int32, (block_len, block_len), 1
        )
        for j in range(blocks):
            t = table[lax.axis_index("ctx") * blocks + j]
            line = pos[:, pl.ds(pl.multiple_of(t * block_len, block_len), block_len)].astype(f32)
            column = jnp.sum(jnp.where(eye, line, 0.0), axis=1, keepdims=True)
            place = lax.broadcasted_iota(jnp.int32, (block_len, 1), 0) + t * block_len
            col_pos[j * block_len : (j + 1) * block_len, :] = column
            col_idx[j * block_len : (j + 1) * block_len, :] = place.astype(f32)
        for k in range(2):
            at = own_rows(k)
            x = hid[at, :].astype(f32)
            normed_o[part(k), :] = (x * rms_scale(x) * gains[0:1, :]).astype(bf16)
            p = col_pos[at, :]
            angle = p * freqs[...]
            cos_o[part(k), :] = jnp.cos(angle)
            sin_o[part(k), :] = jnp.sin(angle)
            idx_o[part(k), :] = col_idx[at, :]
            start_o[part(k), :] = col_idx[at, :] - p
        kv = product(normed_o[...], wkv[...])
        key = kv[:, :head_dim]
        scale = rms_scale(key)
        unit = key * scale
        unit_o[...] = unit
        scale_o[...] = scale
        kv_o[:, :head_dim] = rotate(unit * hgains[1:2, :], cos_o[...], sin_o[...]).astype(bf16)
        kv_o[:, head_dim:] = kv[:, head_dim:].astype(bf16)

    normed, kv_mine, unit_k, scale_k, cosine, sine, idx, start = kernel_call(
        pre_body,
        (block_table, hidden, positions, norm_gains, head_norm_gains, freq, key_value_weight),
        [
            ((rows, width), bf16),
            ((rows, 2 * head_dim), bf16),
            ((rows, head_dim), f32),
            ((rows, 1), f32),
            ((rows, half), f32),
            ((rows, half), f32),
            ((rows, 1), f32),
            ((rows, 1), f32),
        ],
        scratch=[pltpu.VMEM((rows, 1), f32), pltpu.VMEM((rows, 1), f32)],
        tables=1,
    )

    if paired:
        kvs = [kv_mine, other_core(kv_mine)]
    else:
        kvs = [lax.all_gather(kv_mine, "ctx", axis=0, tiled=True)]

    def query_body(nrm, wq, hgains, cos, sin, q_o, unit_o, scale_o):
        raw = product(nrm[...], wq[...])
        for h in range(heads):
            cols = slice(h * head_dim, (h + 1) * head_dim)
            scale = rms_scale(raw[:, cols])
            unit = raw[:, cols] * scale
            unit_o[:, cols] = unit
            scale_o[:, h : h + 1] = scale
            q_o[:, cols] = (rotate(unit * hgains[0:1, :], cos[...], sin[...]) * root).astype(bf16)

    queries, unit_q, scale_q = kernel_call(
        query_body,
        (normed, query_weight, head_norm_gains, cosine, sine),
        [((rows, q_width), bf16), ((rows, q_width), f32), ((rows, heads), f32)],
    )

    def attend_body(*refs):
        table, q, idx_r, start_r, wo = refs[:5]
        kv = refs[5 : 5 + len(kvs)]
        probs_o, context_o, mine_o, send_o = refs[5 + len(kvs) :]
        low = lax.axis_index("tp") & 1
        ctx = lax.axis_index("ctx")
        order = [ctx, ctx ^ 1] if paired else list(range(n_ctx))
        lane = lax.broadcasted_iota(jnp.int32, (1, seq), 1)
        key_idx = lane
        for m, rank in enumerate(order):
            for at in range(0, rows, unit_len):
                first = (low ^ (at // share)) * share + at % share
                base = table[rank * blocks + lax.div(first, block_len)] * block_len
                base = base + lax.rem(first, block_len)
                begin = m * rows + at
                key_idx = jnp.where(
                    (lane >= begin) & (lane < begin + unit_len), lane + (base - begin), key_idx
                )
        key_idx = key_idx.astype(f32)
        allowed = (key_idx <= idx_r[...]) & (key_idx >= start_r[...])
        length = seq // len(kvs)
        for h in range(heads):
            cols = slice(h * head_dim, (h + 1) * head_dim)
            scores = jnp.concatenate(
                [back_product(q[:, cols], r[:, :head_dim]) for r in kv], axis=1
            )
            scores = jnp.where(allowed, scores, -jnp.inf)
            top = jnp.max(scores, axis=1, keepdims=True)
            expo = jnp.exp(scores - top)
            inverse = 1.0 / jnp.sum(expo, axis=1, keepdims=True)
            probs_o[h] = expo * inverse
            probs = expo.astype(bf16)
            mixed = product(probs[:, :length], kv[0][:, head_dim:])
            for m in range(1, len(kvs)):
                mixed = mixed + product(probs[:, m * length : (m + 1) * length], kv[m][:, head_dim:])
            context_o[:, cols] = (mixed * inverse).astype(bf16)
        total = product(context_o[...], wo[...])
        mine_o[...] = total[part(0)]
        send_o[...] = total[part(1)].astype(bf16)

    probs, context, attn_mine, attn_send = kernel_call(
        attend_body,
        (block_table, queries, idx, start, output_weight, *kvs),
        [
            ((heads, rows, seq), f32),
            ((rows, q_width), bf16),
            ((share, width), f32),
            ((share, width), bf16),
        ],
        tables=1,
    )

    def meet_body(a, b, o):
        o[...] = (a[...] + b[...].astype(f32)).astype(bf16)

    def meet(mine, got):
        return kernel_call(meet_body, (mine, got), [((share, width), bf16)])[0]

    attn_met = meet(attn_mine, neighbour(attn_send))
    attn_terms = exchanged(attn_met)
    n_terms = len(attn_terms)
    weights = (gate_weight, up_weight, down_weight, *near_weights)

    def ff_groups(refs):
        return [
            (refs[0][...], refs[1][...], refs[2][...], slice(0, ff)),
            (refs[3][...], refs[4][...], refs[5][...], slice(ff, 2 * ff)),
        ]

    def feed_body(*refs):
        hid, gains = refs[:2]
        groups = ff_groups(refs[2:8])
        attn = summed(refs[8 : 8 + n_terms])
        unit_o, scale_o, mixed_o, x_o, act_o, gate_o, up_o, send_o = refs[8 + n_terms :]
        scale = rms_scale(attn)
        unit = attn * scale
        mixed = hid[own_rows(0), :].astype(f32) + unit * gains[1:2, :]
        unit_o[...] = unit
        scale_o[...] = scale
        mixed_o[...] = mixed
        x = (mixed * rms_scale(mixed) * gains[2:3, :]).astype(bf16)
        x_o[...] = x
        total = None
        for wg, wu, wd, cols in groups:
            gate = product(x, wg)
            up = product(x, wu)
            gate_o[:, cols] = gate
            up_o[:, cols] = up
            inner = gelu_coef * (gate + 0.044715 * gate * gate * gate)
            act = (0.5 * gate * (1.0 + jnp.tanh(inner)) * up).astype(bf16)
            term = product(act, wd)
            total = term if total is None else total + term
            act_o[:, cols] = act
        send_o[...] = total.astype(bf16)

    unit_a, scale_a, mixed, ff_in, activated, gate, up, ff_send = kernel_call(
        feed_body,
        (hidden, norm_gains, *weights, *attn_terms),
        [
            ((share, width), f32),
            ((share, 1), f32),
            ((share, width), f32),
            ((share, width), bf16),
            ((share, 2 * ff), bf16),
            ((share, 2 * ff), f32),
            ((share, 2 * ff), f32),
            ((share, width), bf16),
        ],
    )
    ff_terms = exchanged(ff_send)

    def slope_body(gate_r, up_r, gelu_o, slope_o):
        v = gate_r[...]
        inner = gelu_coef * (v + 0.044715 * v * v * v)
        tanh_val = jnp.tanh(inner)
        gelu_o[...] = 0.5 * v * (1.0 + tanh_val)
        slope = 0.5 * (1.0 + tanh_val) + 0.5 * v * (1.0 - tanh_val * tanh_val) * gelu_coef * (
            1.0 + 3.0 * 0.044715 * v * v
        )
        slope_o[...] = slope * up_r[...]

    gelu, up_slope = kernel_call(slope_body, (gate, up), [((share, 2 * ff), f32), ((share, 2 * ff), f32)])

    def back_body(*refs):
        gains, mixed_r, cot_r, gelu_r, slope_r = refs[:5]
        groups = ff_groups(refs[5:11])
        ff_out = summed(refs[11 : 11 + n_terms])
        hidden_o, gain_o, dout_o, dgate_o, dup_o, send_o = refs[11 + n_terms :]
        scale = rms_scale(ff_out)
        unit = ff_out * scale
        hidden_o[...] = (mixed_r[...] + unit * gains[3:4, :]).astype(bf16)
        grad = cot_r[own_rows(0), :].astype(f32)
        gain_o[...] = jnp.sum(grad * unit, axis=0, keepdims=True) * (1.0 / copies)
        d_out = rms_back(grad, unit, scale, gains[3:4, :]).astype(bf16)
        dout_o[...] = d_out
        total = None
        for wg, wu, wd, cols in groups:
            d_act = back_product(d_out, wd)
            d_gate = (d_act * slope_r[:, cols]).astype(bf16)
            d_up = (d_act * gelu_r[:, cols]).astype(bf16)
            term = back_product(d_gate, wg) + back_product(d_up, wu)
            total = term if total is None else total + term
            dgate_o[:, cols] = d_gate
            dup_o[:, cols] = d_up
        send_o[...] = total.astype(bf16)

    hidden_mine, gain_o, d_ff_out, d_gate, d_up, dff_send = kernel_call(
        back_body,
        (norm_gains, mixed, cot, gelu, up_slope, *weights, *ff_terms),
        [
            ((share, width), bf16),
            ((1, width), f32),
            ((share, width), bf16),
            ((share, 2 * ff), bf16),
            ((share, 2 * ff), bf16),
            ((share, width), bf16),
        ],
    )
    dffin_terms = exchanged(dff_send)
    hidden_near = neighbour(hidden_mine)

    def arrange(acc, outs):
        if not paired:
            outs[0][...] = acc[...]
            return
        batch = lax.axis_index("batch")
        ctx = lax.axis_index("ctx")
        for side in range(2):
            for k in range(n_batch):
                first = ((batch ^ k) * n_ctx + (ctx ^ side)) * out_rows
                outs[side][k * out_rows : (k + 1) * out_rows, :] = acc[
                    pl.ds(pl.multiple_of(first, out_rows), out_rows), :
                ].astype(bf16)

    def grad_call(body, args, columns):
        if paired:
            outs = [((n_batch * out_rows, columns), bf16)] * 2
        else:
            outs = [((width, columns), f32)]
        return kernel_call(body, args, outs, scratch=[pltpu.VMEM((width, columns), f32)])

    def reduce_grads(grads):
        if not paired:
            return [lax.psum_scatter(grads[0], ("batch", "ctx"), scatter_dimension=0, tiled=True)]
        keep, send = grads
        columns = keep.shape[1]
        got = other_core(send)

        def add_body(a, b, *outs):
            total = a[...].astype(f32) + b[...].astype(f32)
            for k in range(n_batch):
                outs[k][...] = total[k * out_rows : (k + 1) * out_rows].astype(outs[k].dtype)

        parts = kernel_call(
            add_body, (keep, got), [((out_rows, columns), f32)] + [((out_rows, columns), bf16)] * (n_batch - 1)
        )
        return [parts[0]] + [swap(parts[k], "batch", n_batch, k) for k in range(1, n_batch)]

    def ff_grad_body(x, d_out, act, dgate, dup, *refs):
        acc = refs[-1]
        for at, left, right in ((0, x, dgate), (1, x, dup), (2, d_out, act)):
            total = lead_product(left[...], right[...])
            acc[:, at * ff : (at + 1) * ff] = total[:, :ff]
            acc[:, (3 + at) * ff : (4 + at) * ff] = total[:, ff:]
        arrange(acc, refs[:-1])

    ff_grads = grad_call(ff_grad_body, (ff_in, d_ff_out, activated, d_gate, d_up), 6 * ff)
    mid_terms = reduce_grads(ff_grads)

    def mix_back_body(gains, mixed_r, unit_r, scale_r, cot_r, *refs):
        d_in = summed(refs[:n_terms])
        dmixed_o, dattn_o, gain_f_o, gain_a_o = refs[n_terms:]
        mixed_v = mixed_r[...]
        scale = rms_scale(mixed_v)
        unit_f = mixed_v * scale
        gain_f_o[...] = jnp.sum(d_in * unit_f, axis=0, keepdims=True) * (1.0 / copies)
        d_mix = cot_r[own_rows(0), :].astype(f32) + rms_back(d_in, unit_f, scale, gains[2:3, :])
        dmixed_o[...] = d_mix
        unit = unit_r[...]
        gain_a_o[...] = jnp.sum(d_mix * unit, axis=0, keepdims=True) * (1.0 / copies)
        dattn_o[...] = rms_back(d_mix, unit, scale_r[...], gains[1:2, :]).astype(bf16)

    d_mixed, dattn_mine, gain_f, gain_a = kernel_call(
        mix_back_body,
        (norm_gains, mixed, unit_a, scale_a, cot, dffin_terms[0], *(after(t, ff_grads[0]) for t in dffin_terms[1:])),
        [((share, width), f32), ((share, width), bf16), ((1, width), f32), ((1, width), f32)],
    )
    d_attn = (dattn_mine, after(neighbour(dattn_mine), mid_terms[0]))

    def attend_back_body(*refs):
        wo, probs_r, q = refs[:3]
        kv = refs[3 : 3 + len(kvs)]
        d_out = joined(refs[3 + len(kvs) : 5 + len(kvs)])
        dq_o = refs[5 + len(kvs)]
        dkv_o = refs[6 + len(kvs) :]
        d_context = back_product(d_out, wo[...]).astype(bf16)
        length = seq // len(kvs)
        for h in range(heads):
            cols = slice(h * head_dim, (h + 1) * head_dim)
            probs_v = probs_r[h]
            d_probs = jnp.concatenate(
                [back_product(d_context[:, cols], r[:, head_dim:]) for r in kv], axis=1
            )
            delta = jnp.sum(probs_v * d_probs, axis=1, keepdims=True)
            d_scores = (probs_v * (d_probs - delta)).astype(bf16)
            rounded = probs_v.astype(bf16)
            d_q = None
            for m, r in enumerate(kv):
                span = slice(m * length, (m + 1) * length)
                term = product(d_scores[:, span], r[:, :head_dim])
                d_q = term if d_q is None else d_q + term
                d_k = lead_product(d_scores[:, span], q[:, cols])
                d_v = lead_product(rounded[:, span], d_context[:, cols])
                if h > 0:
                    d_k = d_k + dkv_o[m][:, :head_dim].astype(f32)
                    d_v = d_v + dkv_o[m][:, head_dim:].astype(f32)
                dkv_o[m][:, :head_dim] = d_k.astype(dkv_o[m].dtype)
                dkv_o[m][:, head_dim:] = d_v.astype(dkv_o[m].dtype)
            dq_o[:, cols] = d_q

    if paired:
        dkv_outs = [((rows, 2 * head_dim), f32), ((rows, 2 * head_dim), f32 if heads > 1 else bf16)]
    else:
        dkv_outs = [((seq, 2 * head_dim), f32)]
    attended_back = kernel_call(
        attend_back_body, (output_weight, probs, queries, *kvs, *d_attn), [((rows, q_width), f32)] + dkv_outs
    )
    d_q = attended_back[0]
    if paired:
        dkv_terms = [attended_back[1], other_core(attended_back[2])]
    else:
        dkv_terms = [lax.psum_scatter(attended_back[1], "ctx", scatter_dimension=0, tiled=True)]

    def query_back_body(dq, unit_r, scale_r, cos, sin, hgains, wq, draw_o, dn_o, gain_o):
        gain = jnp.zeros((1, head_dim), f32)
        for h in range(heads):
            cols = slice(h * head_dim, (h + 1) * head_dim)
            d_unit = rotate_back(dq[:, cols], cos[...], sin[...]) * root
            unit = unit_r[:, cols]
            gain = gain + jnp.sum(d_unit * unit, axis=0, keepdims=True)
            draw_o[:, cols] = rms_back(d_unit, unit, scale_r[:, h : h + 1], hgains[0:1, :]).astype(bf16)
        gain_o[...] = gain
        dn_o[...] = back_product(draw_o[...], wq[...])

    d_query_raw, dn_query, gain_q = kernel_call(
        query_back_body,
        (d_q, unit_q, scale_q, cosine, sine, head_norm_gains, query_weight),
        [((rows, q_width), bf16), ((rows, width), f32), ((1, head_dim), f32)],
    )

    def pre_back_body(dn, unit_r, scale_r, cos, sin, hgains, wkv, *refs):
        count = len(dkv_terms)
        d_kv = summed(refs[:count])
        draw_o, gain_o, mine_o, send_o = refs[count:]
        d_unit = rotate_back(d_kv[:, :head_dim], cos[...], sin[...])
        unit = unit_r[...]
        gain_o[...] = jnp.sum(d_unit * unit, axis=0, keepdims=True)
        draw_o[:, :head_dim] = rms_back(d_unit, unit, scale_r[...], hgains[1:2, :]).astype(bf16)
        draw_o[:, head_dim:] = d_kv[:, head_dim:].astype(bf16)
        total = dn[...] + back_product(draw_o[...], wkv[...])
        mine_o[...] = total[part(0)]
        send_o[...] = total[part(1)].astype(bf16)

    d_kv_raw, gain_k, dn_mine, dn_send = kernel_call(
        pre_back_body,
        (dn_query, unit_k, scale_k, cosine, sine, head_norm_gains, key_value_weight, *dkv_terms),
        [
            ((rows, 2 * head_dim), bf16),
            ((1, head_dim), f32),
            ((share, width), f32),
            ((share, width), bf16),
        ],
    )
    dn_terms = exchanged(meet(dn_mine, neighbour(dn_send)))

    def mid_body(*refs):
        count = len(mid_terms)
        total = summed(refs[:count])
        refs[count][...] = total[:, : 3 * ff]
        refs[count + 1][...] = total[:, 3 * ff :].astype(bf16)

    mid_mine, mid_send = kernel_call(
        mid_body, tuple(mid_terms), [((out_rows, 3 * ff), f32), ((out_rows, 3 * ff), bf16)]
    )

    def ff_out_body(mine, near, *outs):
        for k in range(3):
            cols = slice(k * ff, (k + 1) * ff)
            outs[k][...] = mine[:, cols] + near[:, cols].astype(f32)

    gate_grad, up_grad, down_grad = kernel_call(
        ff_out_body, (mid_mine, neighbour(mid_send)), [((out_rows, ff), f32)] * 3
    )

    lanes = 128
    kv_at = q_width
    gain_at = q_width + 2 * head_dim
    out_at = gain_at + lanes

    def last_grad_body(nrm, draw, dkv, hid, g_o, g_f, g_a, g_q, g_k, mine, send, ctx_r, da, da_near, *refs):
        acc = refs[-1]
        acc[:, :kv_at] = lead_product(nrm[...], draw[...])
        acc[:, out_at:] = lead_product(joined((da, da_near)), ctx_r[...])
        acc[:, kv_at:gain_at] = lead_product(nrm[...], dkv[...])
        g_in = jnp.zeros((1, width), f32)
        for k, terms in enumerate((mine, send)):
            x = hid[own_rows(k), :].astype(f32)
            g_in = g_in + jnp.sum(terms[...].astype(f32) * x * rms_scale(x), axis=0, keepdims=True)
        line = lax.broadcasted_iota(jnp.int32, (lanes, width), 0)
        packed = jnp.where(line == 0, g_in, 0.0)
        for at, row in enumerate((g_a, g_f, g_o), 1):
            packed = jnp.where(line == at, row[...], packed)
        acc[:, gain_at:out_at] = packed.T
        line = lax.broadcasted_iota(jnp.int32, (lanes, head_dim), 0)
        packed = jnp.where(line == 4, g_q[...], jnp.where(line == 5, g_k[...], 0.0)).T
        for d in range(shards):
            at = slice(d * out_rows, d * out_rows + head_rows)
            acc[at, gain_at:out_at] = acc[at, gain_at:out_at] + packed[d * head_rows : (d + 1) * head_rows]
        arrange(acc, refs[:-1])

    last_terms = reduce_grads(
        grad_call(
            last_grad_body,
            (normed, d_query_raw, d_kv_raw, hidden, gain_o, gain_f, gain_a, gain_q, gain_k, dn_mine, dn_send, context, *d_attn),
            out_at + q_width,
        ),
    )

    def last_body(*refs):
        count = len(last_terms)
        total = summed(refs[:count])
        refs[count][...] = total[:, :kv_at]
        refs[count + 1][...] = total[:, kv_at:out_at].astype(bf16)
        refs[count + 2][...] = total[:, out_at:]

    query_grad, kv_mine_sum, out_grad = kernel_call(
        last_body,
        tuple(last_terms),
        [((out_rows, q_width), f32), ((out_rows, 2 * head_dim + lanes), bf16), ((out_rows, q_width), f32)],
    )
    kv_sums = [kv_mine_sum] + [swap(kv_mine_sum, "tp", n_tp, k) for k in range(1, n_tp)]

    def kv_body(*refs):
        terms = [r[...].astype(f32) for r in refs[:n_tp]]
        while len(terms) > 1:
            terms = [a + b for a, b in zip(terms[::2], terms[1::2])]
        refs[n_tp][...] = terms[0][:, : 2 * head_dim]
        lines = terms[0][:, 2 * head_dim :].T
        refs[n_tp + 1][...] = lines[:4]
        refs[n_tp + 2][...] = lines[4:6, :head_rows]

    kv_grad, gain_grad, head_gain_grad = kernel_call(
        kv_body, tuple(kv_sums), [((out_rows, 2 * head_dim), f32), ((4, out_rows), f32), ((2, head_rows), f32)]
    )

    def input_back_body(hid, gains, dmix, *refs):
        d_normed = summed(refs[:n_terms])
        x = hid[own_rows(0), :].astype(f32)
        scale = rms_scale(x)
        refs[n_terms][...] = (dmix[...] + rms_back(d_normed, x * scale, scale, gains[0:1, :])).astype(bf16)

    (input_mine,) = kernel_call(input_back_body, (hidden, norm_gains, d_mixed, *dn_terms), [((share, width), bf16)])

    def place_body(a, b, o):
        o[own_rows(0), :] = a[...]
        o[own_rows(1), :] = b[...]

    def placed(mine, near):
        (whole,) = kernel_call(place_body, (mine, near), [((rows, width), bf16)])
        return whole.reshape(hidden_in.shape)

    return (
        placed(hidden_mine, hidden_near),
        placed(input_mine, neighbour(input_mine)),
        query_grad,
        kv_grad,
        out_grad.T,
        gate_grad,
        up_grad,
        down_grad.T,
        gain_grad,
        head_gain_grad,
    )


def solution(mesh):
    return jax.shard_map(
        on_device,
        mesh=mesh,
        in_specs=(
            P("batch", "ctx", None, None),
            P("batch", None),
            P(),
            P(),
            P(),
            P(None, "tp"),
            P(),
            P("tp", None),
            P(None, "tp"),
            P(None, "tp"),
            P("tp", None),
            P("batch", "ctx", None, None),
        ),
        out_specs=(
            P("batch", "ctx", None, None),
            P("batch", "ctx", None, None),
            P(("batch", "ctx"), "tp"),
            P(("batch", "ctx"), None),
            P("tp", ("batch", "ctx")),
            P(("batch", "ctx"), "tp"),
            P(("batch", "ctx"), "tp"),
            P("tp", ("batch", "ctx")),
            P(None, ("batch", "ctx")),
            P(None, ("batch", "ctx")),
        ),
        check_vma=False,
    )
```

```python
import functools

import jax
import jax.numpy as jnp
import numpy as np
from jax import lax
from jax.experimental import pallas as pl
from jax.experimental.pallas import tpu as pltpu
from jax.sharding import PartitionSpec as P


epsilon = 1e-06
rope_base = 1000000.0
gelu_coef = 0.7978845608028654
f32 = jnp.float32
bf16 = jnp.bfloat16


def rms_scale(v):
    return lax.rsqrt(jnp.mean(v * v, axis=-1, keepdims=True) + epsilon)


def rms_back(grad, unit, scale, gain):
    weighted = grad * gain
    return scale * (weighted - unit * jnp.mean(unit * weighted, axis=-1, keepdims=True))


def rotate(v, cosine, sine):
    half = v.shape[-1] // 2
    first, second = (v[..., :half], v[..., half:])
    return jnp.concatenate(
        [first * cosine - second * sine, second * cosine + first * sine], axis=-1
    )


def rotate_back(g, cosine, sine):
    half = g.shape[-1] // 2
    first, second = (g[..., :half], g[..., half:])
    return jnp.concatenate(
        [first * cosine + second * sine, second * cosine - first * sine], axis=-1
    )


def product(left, right):
    return jnp.dot(left, right, preferred_element_type=f32)


def lead_product(left, right):
    return lax.dot_general(left, right, (((0,), (0,)), ((), ())), preferred_element_type=f32)


def back_product(left, right):
    return lax.dot_general(left, right, (((1,), (1,)), ((), ())), preferred_element_type=f32)


def kernel_call(body, args, outs, scratch=(), tables=0, in_hbm=0):
    moved = sum(a.size * a.dtype.itemsize for a in args)
    moved += sum(functools.reduce(lambda m, n: m * n, s, 1) * jnp.dtype(d).itemsize for s, d in outs)
    work = sum(
        functools.reduce(lambda m, n: m * n, s.shape, 1) * jnp.dtype(s.dtype).itemsize
        for s in scratch
        if s.dtype in (f32, bf16)
    )
    limit = min(60 << 20, (8 << 20) + 2 * (moved + work))
    return pl.pallas_call(
        body,
        out_shape=[jax.ShapeDtypeStruct(s, d) for s, d in outs],
        in_specs=[pl.BlockSpec(memory_space=pltpu.SMEM)] * tables
        + [pl.BlockSpec(memory_space=pltpu.VMEM)] * (len(args) - tables - in_hbm)
        + [pl.BlockSpec(memory_space=pltpu.HBM)] * in_hbm,
        out_specs=[pl.BlockSpec(memory_space=pltpu.VMEM)] * len(outs),
        scratch_shapes=list(scratch),
        cost_estimate=pl.CostEstimate(flops=0, bytes_accessed=moved, transcendentals=0),
        compiler_params=pltpu.CompilerParams(vmem_limit_bytes=limit),
    )(*args)


def swap(x, axis, size, k):
    return lax.ppermute(x, axis, [(i, i ^ k) for i in range(size)])


def after(x, *others):
    return lax.optimization_barrier((x, *others))[0]


def on_device(
    hidden_in,
    positions,
    block_table,
    norm_gains,
    head_norm_gains,
    query_weight,
    key_value_weight,
    output_weight,
    gate_weight,
    up_weight,
    down_weight,
    out_cotangent,
):
    n_tp = lax.axis_size("tp")
    n_ctx = lax.axis_size("ctx")
    n_batch = lax.axis_size("batch")
    blocks, block_len, width = hidden_in.shape[1:]
    rows = blocks * block_len
    head_dim = key_value_weight.shape[1] // 2
    half = head_dim // 2
    heads = query_weight.shape[1] // head_dim
    q_width = heads * head_dim
    ff = gate_weight.shape[1]
    seq = positions.shape[1]
    root = head_dim ** (-0.5)
    share = rows // 2
    unit_len = min(share, block_len)
    peers = tuple(range(2, n_tp, 2))
    copies = n_tp // 2
    shards = n_batch * n_ctx
    out_rows = width // shards
    head_rows = head_dim // shards
    paired = n_ctx == 2 and n_batch in (2, 4)

    hidden = hidden_in.reshape(rows, width)
    cot = out_cotangent.reshape(rows, width)
    freq = jnp.asarray(rope_base ** (-np.arange(half) * 2.0 / head_dim), f32).reshape(1, half)

    def part(k):
        return slice(k * share, (k + 1) * share)

    def own_rows(k):
        return pl.ds(pl.multiple_of(((lax.axis_index("tp") & 1) ^ k) * share, share), share)

    def neighbour(x):
        return swap(x, "tp", n_tp, 1)

    def other_core(x):
        return swap(x, "ctx", n_ctx, 1)

    def exchanged(x):
        return [x] + [swap(x, "tp", n_tp, k) for k in peers]

    def joined(refs, columns=slice(None)):
        return jnp.concatenate([r[:, columns] for r in refs], axis=0)

    def summed(refs):
        total = refs[0][...].astype(f32)
        for r in refs[1:]:
            total = total + r[...].astype(f32)
        return total

    def own_half(length):
        half_length = length // 2
        return pl.ds(pl.multiple_of((lax.axis_index("ctx") & 1) * half_length, half_length), half_length)

    def own_piece(length):
        piece = length // (2 * n_batch)
        place = ((lax.axis_index("ctx") & 1) * n_batch + lax.axis_index("batch")) * piece
        return pl.ds(pl.multiple_of(place, piece), piece)

    up_piece = width // (2 * n_batch)
    down_piece = ff // (2 * n_batch)
    piece_rows = max(up_piece, down_piece)

    def pre_body(*refs):
        sources, (gate, up, down) = refs[:7], refs[7:10]
        normed_o, kv_o, unit_o, scale_o, cos_o, sin_o, idx_o, start_o, gate_o, piece_o = refs[10:20]
        col_pos, col_idx, sem = refs[20:23]
        table, hid, pos, gains, hgains, freqs, wkv = refs[23:]
        loads = [pltpu.make_async_copy(a, b, sem.at[i]) for i, (a, b) in enumerate(zip(sources, refs[23:]))]
        moves = [
            pltpu.make_async_copy(up.at[own_piece(width), :], piece_o.at[:up_piece, :ff], sem.at[7]),
            pltpu.make_async_copy(down.at[own_piece(ff), :], piece_o.at[:down_piece, ff:], sem.at[8]),
            pltpu.make_async_copy(gate.at[own_half(width), :], gate_o, sem.at[9]),
        ]
        for move in loads + moves:
            move.start()
        if up_piece < piece_rows:
            piece_o[up_piece:, :ff] = jnp.zeros((piece_rows - up_piece, ff), bf16)
        if down_piece < piece_rows:
            piece_o[down_piece:, ff:] = jnp.zeros((piece_rows - down_piece, width), bf16)
        for load in loads:
            load.wait()
        eye = lax.broadcasted_iota(jnp.int32, (block_len, block_len), 0) == lax.broadcasted_iota(
            jnp.int32, (block_len, block_len), 1
        )
        for j in range(blocks):
            t = table[lax.axis_index("ctx") * blocks + j]
            line = pos[:, pl.ds(pl.multiple_of(t * block_len, block_len), block_len)].astype(f32)
            column = jnp.sum(jnp.where(eye, line, 0.0), axis=1, keepdims=True)
            place = lax.broadcasted_iota(jnp.int32, (block_len, 1), 0) + t * block_len
            col_pos[j * block_len : (j + 1) * block_len, :] = column
            col_idx[j * block_len : (j + 1) * block_len, :] = place.astype(f32)
        for k in range(2):
            at = own_rows(k)
            x = hid[at, :].astype(f32)
            normed_o[part(k), :] = (x * rms_scale(x) * gains[0:1, :]).astype(bf16)
            p = col_pos[at, :]
            angle = p * freqs[...]
            cos_o[part(k), :] = jnp.cos(angle)
            sin_o[part(k), :] = jnp.sin(angle)
            idx_o[part(k), :] = col_idx[at, :]
            start_o[part(k), :] = col_idx[at, :] - p
        kv = product(normed_o[...], wkv[...])
        key = kv[:, :head_dim]
        scale = rms_scale(key)
        unit = key * scale
        unit_o[...] = unit
        scale_o[...] = scale
        kv_o[:, :head_dim] = rotate(unit * hgains[1:2, :], cos_o[...], sin_o[...]).astype(bf16)
        kv_o[:, head_dim:] = kv[:, head_dim:].astype(bf16)
        for move in moves:
            move.wait()

    sources = (block_table, hidden, positions, norm_gains, head_norm_gains, freq, key_value_weight)
    normed, kv_mine, unit_k, scale_k, cosine, sine, idx, start, gate_pack, piece_pack = kernel_call(
        pre_body,
        tuple(
            pltpu.with_memory_space_constraint(x, pltpu.HBM)
            for x in (*sources, gate_weight, up_weight, down_weight)
        ),
        [
            ((rows, width), bf16),
            ((rows, 2 * head_dim), bf16),
            ((rows, head_dim), f32),
            ((rows, 1), f32),
            ((rows, half), f32),
            ((rows, half), f32),
            ((rows, 1), f32),
            ((rows, 1), f32),
            ((width // 2, ff), bf16),
            ((piece_rows, ff + width), bf16),
        ],
        scratch=[pltpu.VMEM((rows, 1), f32), pltpu.VMEM((rows, 1), f32), pltpu.SemaphoreType.DMA((10,))]
        + [pltpu.SMEM(block_table.shape, block_table.dtype)]
        + [pltpu.VMEM(x.shape, x.dtype) for x in sources[1:]],
        in_hbm=10,
    )

    gate_near = neighbour(gate_pack)
    piece_near = neighbour(piece_pack)
    pieces = [piece_near] + [swap(piece_near, "batch", n_batch, k) for k in range(1, n_batch)]

    def stack_body(*refs):
        up_o, down_o = refs[n_batch:]
        for k in range(n_batch):
            b = lax.axis_index("batch") ^ k
            up_o[pl.ds(pl.multiple_of(b * up_piece, up_piece), up_piece), :] = refs[k][:up_piece, :ff]
            down_o[pl.ds(pl.multiple_of(b * down_piece, down_piece), down_piece), :] = refs[k][
                :down_piece, ff:
            ]

    up_near, down_near = kernel_call(stack_body, tuple(pieces), [((width // 2, ff), bf16), ((ff // 2, width), bf16)])

    def whole_body(*refs):
        for mine, far, whole in zip(refs[:3], refs[3:6], refs[6:]):
            length = mine.shape[0]
            for k, ref in enumerate((mine, far)):
                place = ((lax.axis_index("ctx") & 1) ^ k) * length
                whole[pl.ds(pl.multiple_of(place, length), length), :] = ref[...]

    halves = (gate_near, up_near, down_near)
    near_weights = kernel_call(
        whole_body,
        halves + tuple(other_core(h) for h in halves),
        [((width, ff), bf16), ((width, ff), bf16), ((ff, width), bf16)],
    )

    if paired:
        kvs = [kv_mine, other_core(kv_mine)]
    else:
        kvs = [lax.all_gather(kv_mine, "ctx", axis=0, tiled=True)]

    def query_body(nrm, wq, hgains, cos, sin, q_o, unit_o, scale_o):
        raw = product(nrm[...], wq[...])
        for h in range(heads):
            cols = slice(h * head_dim, (h + 1) * head_dim)
            scale = rms_scale(raw[:, cols])
            unit = raw[:, cols] * scale
            unit_o[:, cols] = unit
            scale_o[:, h : h + 1] = scale
            q_o[:, cols] = (rotate(unit * hgains[0:1, :], cos[...], sin[...]) * root).astype(bf16)

    queries, unit_q, scale_q = kernel_call(
        query_body,
        (normed, query_weight, head_norm_gains, cosine, sine),
        [((rows, q_width), bf16), ((rows, q_width), f32), ((rows, heads), f32)],
    )

    def attend_body(*refs):
        table, q, idx_r, start_r, wo = refs[:5]
        kv = refs[5 : 5 + len(kvs)]
        probs_o, context_o, mine_o, send_o = refs[5 + len(kvs) :]
        low = lax.axis_index("tp") & 1
        ctx = lax.axis_index("ctx")
        order = [ctx, ctx ^ 1] if paired else list(range(n_ctx))
        lane = lax.broadcasted_iota(jnp.int32, (1, seq), 1)
        key_idx = lane
        for m, rank in enumerate(order):
            for at in range(0, rows, unit_len):
                first = (low ^ (at // share)) * share + at % share
                base = table[rank * blocks + lax.div(first, block_len)] * block_len
                base = base + lax.rem(first, block_len)
                begin = m * rows + at
                key_idx = jnp.where(
                    (lane >= begin) & (lane < begin + unit_len), lane + (base - begin), key_idx
                )
        key_idx = key_idx.astype(f32)
        allowed = (key_idx <= idx_r[...]) & (key_idx >= start_r[...])
        length = seq // len(kvs)
        for h in range(heads):
            cols = slice(h * head_dim, (h + 1) * head_dim)
            scores = jnp.concatenate(
                [back_product(q[:, cols], r[:, :head_dim]) for r in kv], axis=1
            )
            scores = jnp.where(allowed, scores, -jnp.inf)
            top = jnp.max(scores, axis=1, keepdims=True)
            expo = jnp.exp(scores - top)
            inverse = 1.0 / jnp.sum(expo, axis=1, keepdims=True)
            probs_o[h] = expo * inverse
            probs = expo.astype(bf16)
            mixed = product(probs[:, :length], kv[0][:, head_dim:])
            for m in range(1, len(kvs)):
                mixed = mixed + product(probs[:, m * length : (m + 1) * length], kv[m][:, head_dim:])
            context_o[:, cols] = (mixed * inverse).astype(bf16)
        total = product(context_o[...], wo[...])
        mine_o[...] = total[part(0)]
        send_o[...] = total[part(1)].astype(bf16)

    probs, context, attn_mine, attn_send = kernel_call(
        attend_body,
        (block_table, queries, idx, start, output_weight, *kvs),
        [
            ((heads, rows, seq), f32),
            ((rows, q_width), bf16),
            ((share, width), f32),
            ((share, width), bf16),
        ],
        tables=1,
    )

    def meet_body(a, b, o):
        o[...] = (a[...] + b[...].astype(f32)).astype(bf16)

    def meet(mine, got):
        return kernel_call(meet_body, (mine, got), [((share, width), bf16)])[0]

    attn_met = meet(attn_mine, neighbour(attn_send))
    attn_terms = exchanged(attn_met)
    n_terms = len(attn_terms)
    weights = (gate_weight, up_weight, down_weight, *near_weights)

    def ff_groups(refs):
        return [
            (refs[0][...], refs[1][...], refs[2][...], slice(0, ff)),
            (refs[3][...], refs[4][...], refs[5][...], slice(ff, 2 * ff)),
        ]

    def feed_body(*refs):
        hid, gains = refs[:2]
        groups = ff_groups(refs[2:8])
        attn = summed(refs[8 : 8 + n_terms])
        unit_o, scale_o, mixed_o, x_o = refs[8 + n_terms : 12 + n_terms]
        act_o = refs[12 + n_terms : 14 + n_terms]
        gate_o, up_o, send_o = refs[14 + n_terms :]
        scale = rms_scale(attn)
        unit = attn * scale
        mixed = hid[own_rows(0), :].astype(f32) + unit * gains[1:2, :]
        unit_o[...] = unit
        scale_o[...] = scale
        mixed_o[...] = mixed
        x = (mixed * rms_scale(mixed) * gains[2:3, :]).astype(bf16)
        x_o[...] = x
        total = None
        for k, (wg, wu, wd, cols) in enumerate(groups):
            gate = product(x, wg)
            up = product(x, wu)
            gate_o[:, cols] = gate
            up_o[:, cols] = up
            inner = gelu_coef * (gate + 0.044715 * gate * gate * gate)
            act = (0.5 * gate * (1.0 + jnp.tanh(inner)) * up).astype(bf16)
            term = product(act, wd)
            total = term if total is None else total + term
            act_o[k][...] = act
        send_o[...] = total.astype(bf16)

    unit_a, scale_a, mixed, ff_in, act_mine, act_send, gate, up, ff_send = kernel_call(
        feed_body,
        (hidden, norm_gains, *weights, *attn_terms),
        [
            ((share, width), f32),
            ((share, 1), f32),
            ((share, width), f32),
            ((share, width), bf16),
            ((share, ff), bf16),
            ((share, ff), bf16),
            ((share, 2 * ff), f32),
            ((share, 2 * ff), f32),
            ((share, width), bf16),
        ],
    )
    ff_terms = exchanged(ff_send)
    act_near = neighbour(act_send)

    def slope_body(gate_r, up_r, gelu_o, slope_o):
        v = gate_r[...]
        inner = gelu_coef * (v + 0.044715 * v * v * v)
        tanh_val = jnp.tanh(inner)
        gelu_o[...] = 0.5 * v * (1.0 + tanh_val)
        slope = 0.5 * (1.0 + tanh_val) + 0.5 * v * (1.0 - tanh_val * tanh_val) * gelu_coef * (
            1.0 + 3.0 * 0.044715 * v * v
        )
        slope_o[...] = slope * up_r[...]

    gelu, up_slope = kernel_call(slope_body, (gate, up), [((share, 2 * ff), f32), ((share, 2 * ff), f32)])

    def back_body(*refs):
        gains, mixed_r, cot_r, gelu_r, slope_r = refs[:5]
        groups = ff_groups(refs[5:11])
        ff_out = summed(refs[11 : 11 + n_terms])
        hidden_o, gain_o, dout_o, dgate_o, dup_o, send_o = refs[11 + n_terms :]
        scale = rms_scale(ff_out)
        unit = ff_out * scale
        hidden_o[...] = (mixed_r[...] + unit * gains[3:4, :]).astype(bf16)
        grad = cot_r[own_rows(0), :].astype(f32)
        gain_o[...] = jnp.sum(grad * unit, axis=0, keepdims=True) * (1.0 / copies)
        d_out = rms_back(grad, unit, scale, gains[3:4, :]).astype(bf16)
        dout_o[...] = d_out
        total = None
        for wg, wu, wd, cols in groups:
            d_act = back_product(d_out, wd)
            d_gate = (d_act * slope_r[:, cols]).astype(bf16)
            d_up = (d_act * gelu_r[:, cols]).astype(bf16)
            term = back_product(d_gate, wg) + back_product(d_up, wu)
            total = term if total is None else total + term
            dgate_o[:, cols] = d_gate
            dup_o[:, cols] = d_up
        send_o[...] = total.astype(bf16)

    hidden_mine, gain_o, d_ff_out, d_gate, d_up, dff_send = kernel_call(
        back_body,
        (norm_gains, mixed, cot, gelu, up_slope, *weights, *ff_terms),
        [
            ((share, width), bf16),
            ((1, width), f32),
            ((share, width), bf16),
            ((share, 2 * ff), bf16),
            ((share, 2 * ff), bf16),
            ((share, width), bf16),
        ],
    )
    dffin_terms = exchanged(dff_send)
    hidden_near = neighbour(hidden_mine)
    d_ff_near = neighbour(d_ff_out)

    def arrange(acc, outs):
        if not paired:
            outs[0][...] = acc[...]
            return
        batch = lax.axis_index("batch")
        ctx = lax.axis_index("ctx")
        for side in range(2):
            for k in range(n_batch):
                first = ((batch ^ k) * n_ctx + (ctx ^ side)) * out_rows
                outs[side][k * out_rows : (k + 1) * out_rows, :] = acc[
                    pl.ds(pl.multiple_of(first, out_rows), out_rows), :
                ].astype(bf16)

    def grad_call(fill, args, *columns):
        count = 2 if paired else 1

        def body(*refs):
            accs = refs[len(args) + count * len(columns) :]
            fill(*refs[: len(args)], *accs)
            for k, acc in enumerate(accs):
                at = len(args) + count * k
                arrange(acc, refs[at : at + count])

        outs = []
        for c in columns:
            outs += [((n_batch * out_rows, c), bf16)] * 2 if paired else [((width, c), f32)]
        terms = kernel_call(body, args, outs, scratch=[pltpu.VMEM((width, c), f32) for c in columns])
        return [terms[count * k : count * (k + 1)] for k in range(len(columns))]

    def reduce_grads(*grads):
        if not paired:
            sums = [
                lax.psum_scatter(g[0], ("batch", "ctx"), scatter_dimension=0, tiled=True) for g in grads
            ]
            return [jnp.concatenate(sums, axis=1)]
        columns = sum(g[0].shape[1] for g in grads)
        pairs = [x for keep, send in grads for x in (keep, other_core(send))]

        def add_body(*refs):
            at = 0
            for a, b in zip(refs[: len(pairs) : 2], refs[1 : len(pairs) : 2]):
                total = a[...].astype(f32) + b[...].astype(f32)
                cols = slice(at, at + total.shape[1])
                at = cols.stop
                for k, out in enumerate(refs[len(pairs) :]):
                    out[:, cols] = total[k * out_rows : (k + 1) * out_rows].astype(out.dtype)

        parts = kernel_call(
            add_body, tuple(pairs), [((out_rows, columns), f32)] + [((out_rows, columns), bf16)] * (n_batch - 1)
        )
        return [parts[0]] + [swap(parts[k], "batch", n_batch, k) for k in range(1, n_batch)]

    def ff_grad_fill(x, dgate, dup, near_acc, own_acc):
        for at, right in enumerate((dgate, dup)):
            total = lead_product(x[...], right[...])
            own_acc[:, at * ff : (at + 1) * ff] = total[:, :ff]
            near_acc[:, at * ff : (at + 1) * ff] = total[:, ff:]

    near_grads, own_grads = grad_call(ff_grad_fill, (ff_in, d_gate, d_up), 2 * ff, 2 * ff)
    mid_terms = reduce_grads(near_grads)

    def mix_back_body(gains, mixed_r, unit_r, scale_r, cot_r, *refs):
        d_in = summed(refs[:n_terms])
        dmixed_o, dattn_o, gain_f_o, gain_a_o = refs[n_terms:]
        mixed_v = mixed_r[...]
        scale = rms_scale(mixed_v)
        unit_f = mixed_v * scale
        gain_f_o[...] = jnp.sum(d_in * unit_f, axis=0, keepdims=True) * (1.0 / copies)
        d_mix = cot_r[own_rows(0), :].astype(f32) + rms_back(d_in, unit_f, scale, gains[2:3, :])
        dmixed_o[...] = d_mix
        unit = unit_r[...]
        gain_a_o[...] = jnp.sum(d_mix * unit, axis=0, keepdims=True) * (1.0 / copies)
        dattn_o[...] = rms_back(d_mix, unit, scale_r[...], gains[1:2, :]).astype(bf16)

    d_mixed, dattn_mine, gain_f, gain_a = kernel_call(
        mix_back_body,
        (norm_gains, mixed, unit_a, scale_a, cot, dffin_terms[0], *(after(t, near_grads[0]) for t in dffin_terms[1:])),
        [((share, width), f32), ((share, width), bf16), ((1, width), f32), ((1, width), f32)],
    )
    d_attn = (dattn_mine, after(neighbour(dattn_mine), mid_terms[0]))

    def attend_back_body(*refs):
        wo, probs_r, q = refs[:3]
        kv = refs[3 : 3 + len(kvs)]
        d_out = joined(refs[3 + len(kvs) : 5 + len(kvs)])
        dq_o = refs[5 + len(kvs)]
        dkv_o = refs[6 + len(kvs) :]
        d_context = back_product(d_out, wo[...]).astype(bf16)
        length = seq // len(kvs)
        for h in range(heads):
            cols = slice(h * head_dim, (h + 1) * head_dim)
            probs_v = probs_r[h]
            d_probs = jnp.concatenate(
                [back_product(d_context[:, cols], r[:, head_dim:]) for r in kv], axis=1
            )
            delta = jnp.sum(probs_v * d_probs, axis=1, keepdims=True)
            d_scores = (probs_v * (d_probs - delta)).astype(bf16)
            rounded = probs_v.astype(bf16)
            d_q = None
            for m, r in enumerate(kv):
                span = slice(m * length, (m + 1) * length)
                term = product(d_scores[:, span], r[:, :head_dim])
                d_q = term if d_q is None else d_q + term
                d_k = lead_product(d_scores[:, span], q[:, cols])
                d_v = lead_product(rounded[:, span], d_context[:, cols])
                if h > 0:
                    d_k = d_k + dkv_o[m][:, :head_dim].astype(f32)
                    d_v = d_v + dkv_o[m][:, head_dim:].astype(f32)
                dkv_o[m][:, :head_dim] = d_k.astype(dkv_o[m].dtype)
                dkv_o[m][:, head_dim:] = d_v.astype(dkv_o[m].dtype)
            dq_o[:, cols] = d_q

    if paired:
        dkv_outs = [((rows, 2 * head_dim), f32), ((rows, 2 * head_dim), f32 if heads > 1 else bf16)]
    else:
        dkv_outs = [((seq, 2 * head_dim), f32)]
    attended_back = kernel_call(
        attend_back_body, (output_weight, probs, queries, *kvs, *d_attn), [((rows, q_width), f32)] + dkv_outs
    )
    d_q = attended_back[0]
    if paired:
        dkv_terms = [attended_back[1], other_core(attended_back[2])]
    else:
        dkv_terms = [lax.psum_scatter(attended_back[1], "ctx", scatter_dimension=0, tiled=True)]

    def query_back_body(dq, unit_r, scale_r, cos, sin, hgains, wq, draw_o, dn_o, gain_o):
        gain = jnp.zeros((1, head_dim), f32)
        for h in range(heads):
            cols = slice(h * head_dim, (h + 1) * head_dim)
            d_unit = rotate_back(dq[:, cols], cos[...], sin[...]) * root
            unit = unit_r[:, cols]
            gain = gain + jnp.sum(d_unit * unit, axis=0, keepdims=True)
            draw_o[:, cols] = rms_back(d_unit, unit, scale_r[:, h : h + 1], hgains[0:1, :]).astype(bf16)
        gain_o[...] = gain
        dn_o[...] = back_product(draw_o[...], wq[...])

    d_query_raw, dn_query, gain_q = kernel_call(
        query_back_body,
        (d_q, unit_q, scale_q, cosine, sine, head_norm_gains, query_weight),
        [((rows, q_width), bf16), ((rows, width), f32), ((1, head_dim), f32)],
    )

    def pre_back_body(dn, unit_r, scale_r, cos, sin, hgains, wkv, *refs):
        count = len(dkv_terms)
        d_kv = summed(refs[:count])
        draw_o, gain_o, mine_o, send_o = refs[count:]
        d_unit = rotate_back(d_kv[:, :head_dim], cos[...], sin[...])
        unit = unit_r[...]
        gain_o[...] = jnp.sum(d_unit * unit, axis=0, keepdims=True)
        draw_o[:, :head_dim] = rms_back(d_unit, unit, scale_r[...], hgains[1:2, :]).astype(bf16)
        draw_o[:, head_dim:] = d_kv[:, head_dim:].astype(bf16)
        total = dn[...] + back_product(draw_o[...], wkv[...])
        mine_o[...] = total[part(0)]
        send_o[...] = total[part(1)].astype(bf16)

    d_kv_raw, gain_k, dn_mine, dn_send = kernel_call(
        pre_back_body,
        (dn_query, unit_k, scale_k, cosine, sine, head_norm_gains, key_value_weight, *dkv_terms),
        [
            ((rows, 2 * head_dim), bf16),
            ((1, head_dim), f32),
            ((share, width), f32),
            ((share, width), bf16),
        ],
    )
    dn_terms = exchanged(meet(dn_mine, neighbour(dn_send)))

    def mid_body(*refs):
        refs[-1][...] = summed(refs[:-1]).astype(bf16)

    (mid_send,) = kernel_call(mid_body, tuple(mid_terms), [((out_rows, 2 * ff), bf16)])
    mid_near = neighbour(mid_send)

    def down_grad_fill(dff, dff_near, act, act_r, acc):
        acc[...] = lead_product(joined((dff, dff_near)), joined((act, act_r)))

    def out_grad_fill(da, da_near, ctx_r, acc):
        acc[...] = lead_product(joined((da, da_near)), ctx_r[...])

    side_terms = reduce_grads(
        own_grads,
        *grad_call(down_grad_fill, (d_ff_out, d_ff_near, act_mine, act_near), ff),
        *grad_call(out_grad_fill, (*d_attn, context), q_width),
    )

    def side_body(*refs):
        total = summed(refs[: len(side_terms)])
        near, gate_o, up_o, down_o, out_o = refs[len(side_terms) :]
        gate_o[...] = total[:, :ff] + near[:, :ff].astype(f32)
        up_o[...] = total[:, ff : 2 * ff] + near[:, ff:].astype(f32)
        down_o[...] = total[:, 2 * ff : 3 * ff]
        out_o[...] = total[:, 3 * ff :]

    gate_grad, up_grad, down_grad, out_grad = kernel_call(
        side_body, (*side_terms, mid_near), [((out_rows, ff), f32)] * 3 + [((out_rows, q_width), f32)]
    )

    lanes = 128
    kv_at = q_width
    gain_at = q_width + 2 * head_dim

    def last_grad_fill(nrm, draw, dkv, hid, g_o, g_f, g_a, g_q, g_k, mine, send, acc):
        acc[:, :kv_at] = lead_product(nrm[...], draw[...])
        acc[:, kv_at:gain_at] = lead_product(nrm[...], dkv[...])
        g_in = jnp.zeros((1, width), f32)
        for k, terms in enumerate((mine, send)):
            x = hid[own_rows(k), :].astype(f32)
            g_in = g_in + jnp.sum(terms[...].astype(f32) * x * rms_scale(x), axis=0, keepdims=True)
        line = lax.broadcasted_iota(jnp.int32, (lanes, width), 0)
        packed = jnp.where(line == 0, g_in, 0.0)
        for at, row in enumerate((g_a, g_f, g_o), 1):
            packed = jnp.where(line == at, row[...], packed)
        acc[:, gain_at:] = packed.T
        line = lax.broadcasted_iota(jnp.int32, (lanes, head_dim), 0)
        packed = jnp.where(line == 4, g_q[...], jnp.where(line == 5, g_k[...], 0.0)).T
        for d in range(shards):
            at = slice(d * out_rows, d * out_rows + head_rows)
            acc[at, gain_at:] = acc[at, gain_at:] + packed[d * head_rows : (d + 1) * head_rows]

    last_terms = reduce_grads(
        *grad_call(
            last_grad_fill,
            (normed, d_query_raw, d_kv_raw, hidden, gain_o, gain_f, gain_a, gain_q, gain_k, dn_mine, dn_send),
            gain_at + lanes,
        ),
    )

    def last_body(*refs):
        count = len(last_terms)
        total = summed(refs[:count])
        refs[count][...] = total[:, :kv_at]
        refs[count + 1][...] = total[:, kv_at:].astype(bf16)

    query_grad, kv_mine_sum = kernel_call(
        last_body, tuple(last_terms), [((out_rows, q_width), f32), ((out_rows, 2 * head_dim + lanes), bf16)]
    )
    kv_sums = [kv_mine_sum] + [swap(kv_mine_sum, "tp", n_tp, k) for k in range(1, n_tp)]

    def kv_body(*refs):
        terms = [r[...].astype(f32) for r in refs[:n_tp]]
        while len(terms) > 1:
            terms = [a + b for a, b in zip(terms[::2], terms[1::2])]
        refs[n_tp][...] = terms[0][:, : 2 * head_dim]
        lines = terms[0][:, 2 * head_dim :].T
        refs[n_tp + 1][...] = lines[:4]
        refs[n_tp + 2][...] = lines[4:6, :head_rows]

    kv_grad, gain_grad, head_gain_grad = kernel_call(
        kv_body, tuple(kv_sums), [((out_rows, 2 * head_dim), f32), ((4, out_rows), f32), ((2, head_rows), f32)]
    )

    def input_back_body(hid, gains, dmix, *refs):
        d_normed = summed(refs[:n_terms])
        x = hid[own_rows(0), :].astype(f32)
        scale = rms_scale(x)
        refs[n_terms][...] = (dmix[...] + rms_back(d_normed, x * scale, scale, gains[0:1, :])).astype(bf16)

    (input_mine,) = kernel_call(input_back_body, (hidden, norm_gains, d_mixed, *dn_terms), [((share, width), bf16)])

    def place_body(a, b, o):
        o[own_rows(0), :] = a[...]
        o[own_rows(1), :] = b[...]

    def placed(mine, near):
        (whole,) = kernel_call(place_body, (mine, near), [((rows, width), bf16)])
        return whole.reshape(hidden_in.shape)

    return (
        placed(hidden_mine, hidden_near),
        placed(input_mine, neighbour(input_mine)),
        query_grad,
        kv_grad,
        out_grad.T,
        gate_grad,
        up_grad,
        down_grad.T,
        gain_grad,
        head_gain_grad,
    )


def solution(mesh):
    return jax.shard_map(
        on_device,
        mesh=mesh,
        in_specs=(
            P("batch", "ctx", None, None),
            P("batch", None),
            P(),
            P(),
            P(),
            P(None, "tp"),
            P(),
            P("tp", None),
            P(None, "tp"),
            P(None, "tp"),
            P("tp", None),
            P("batch", "ctx", None, None),
        ),
        out_specs=(
            P("batch", "ctx", None, None),
            P("batch", "ctx", None, None),
            P(("batch", "ctx"), "tp"),
            P(("batch", "ctx"), None),
            P("tp", ("batch", "ctx")),
            P(("batch", "ctx"), "tp"),
            P(("batch", "ctx"), "tp"),
            P("tp", ("batch", "ctx")),
            P(None, ("batch", "ctx")),
            P(None, ("batch", "ctx")),
        ),
        check_vma=False,
    )
```

```python
import functools

import jax
import jax.numpy as jnp
import numpy as np
from jax import lax
from jax.experimental import pallas as pl
from jax.experimental.pallas import tpu as pltpu
from jax.sharding import PartitionSpec as P


epsilon = 1e-06
rope_base = 1000000.0
gelu_coef = 0.7978845608028654
f32 = jnp.float32
bf16 = jnp.bfloat16


def rms_scale(v):
    return lax.rsqrt(jnp.mean(v * v, axis=-1, keepdims=True) + epsilon)


def rms_back(grad, unit, scale, gain):
    weighted = grad * gain
    return scale * (weighted - unit * jnp.mean(unit * weighted, axis=-1, keepdims=True))


def rotate(v, cosine, sine):
    half = v.shape[-1] // 2
    first, second = (v[..., :half], v[..., half:])
    return jnp.concatenate(
        [first * cosine - second * sine, second * cosine + first * sine], axis=-1
    )


def rotate_back(g, cosine, sine):
    half = g.shape[-1] // 2
    first, second = (g[..., :half], g[..., half:])
    return jnp.concatenate(
        [first * cosine + second * sine, second * cosine - first * sine], axis=-1
    )


def product(left, right):
    return jnp.dot(left, right, preferred_element_type=f32)


def lead_product(left, right):
    return lax.dot_general(left, right, (((0,), (0,)), ((), ())), preferred_element_type=f32)


def back_product(left, right):
    return lax.dot_general(left, right, (((1,), (1,)), ((), ())), preferred_element_type=f32)


def kernel_call(body, args, outs, scratch=(), tables=0, in_hbm=0):
    moved = sum(a.size * a.dtype.itemsize for a in args)
    moved += sum(functools.reduce(lambda m, n: m * n, s, 1) * jnp.dtype(d).itemsize for s, d in outs)
    work = sum(
        functools.reduce(lambda m, n: m * n, s.shape, 1) * jnp.dtype(s.dtype).itemsize
        for s in scratch
        if s.dtype in (f32, bf16)
    )
    limit = min(60 << 20, (8 << 20) + 2 * (moved + work))
    return pl.pallas_call(
        body,
        out_shape=[jax.ShapeDtypeStruct(s, d) for s, d in outs],
        in_specs=[pl.BlockSpec(memory_space=pltpu.SMEM)] * tables
        + [pl.BlockSpec(memory_space=pltpu.VMEM)] * (len(args) - tables - in_hbm)
        + [pl.BlockSpec(memory_space=pltpu.HBM)] * in_hbm,
        out_specs=[pl.BlockSpec(memory_space=pltpu.VMEM)] * len(outs),
        scratch_shapes=list(scratch),
        cost_estimate=pl.CostEstimate(flops=0, bytes_accessed=moved, transcendentals=0),
        compiler_params=pltpu.CompilerParams(vmem_limit_bytes=limit),
    )(*args)


def swap(x, axis, size, k):
    return lax.ppermute(x, axis, [(i, i ^ k) for i in range(size)])


def after(x, *others):
    return lax.optimization_barrier((x, *others))[0]


def on_device(
    hidden_in,
    positions,
    block_table,
    norm_gains,
    head_norm_gains,
    query_weight,
    key_value_weight,
    output_weight,
    gate_weight,
    up_weight,
    down_weight,
    out_cotangent,
):
    n_tp = lax.axis_size("tp")
    n_ctx = lax.axis_size("ctx")
    n_batch = lax.axis_size("batch")
    blocks, block_len, width = hidden_in.shape[1:]
    rows = blocks * block_len
    head_dim = key_value_weight.shape[1] // 2
    half = head_dim // 2
    heads = query_weight.shape[1] // head_dim
    q_width = heads * head_dim
    ff = gate_weight.shape[1]
    seq = positions.shape[1]
    root = head_dim ** (-0.5)
    share = rows // 2
    streams = 2
    piece = share // streams
    unit_len = min(share, block_len)
    peers = tuple(range(2, n_tp, 2))
    copies = n_tp // 2
    shards = n_batch * n_ctx
    out_rows = width // shards
    head_rows = head_dim // shards
    paired = n_ctx == 2 and n_batch in (2, 4)

    hidden = hidden_in.reshape(rows, width)
    cot = out_cotangent.reshape(rows, width)
    freq = jnp.asarray(rope_base ** (-np.arange(half) * 2.0 / head_dim), f32).reshape(1, half)

    def part(k):
        return slice(k * share, (k + 1) * share)

    def own_rows(k):
        return pl.ds(pl.multiple_of(((lax.axis_index("tp") & 1) ^ k) * share, share), share)

    def own_stream(k):
        place = (lax.axis_index("tp") & 1) * share + k * piece
        return pl.ds(pl.multiple_of(place, piece), piece)

    def neighbour(x):
        return swap(x, "tp", n_tp, 1)

    def other_core(x):
        return swap(x, "ctx", n_ctx, 1)

    def exchanged(x):
        return [x] + [swap(x, "tp", n_tp, k) for k in peers]

    def joined(refs, columns=slice(None)):
        return jnp.concatenate([r[:, columns] for r in refs], axis=0)

    def summed(refs):
        total = refs[0][...].astype(f32)
        for r in refs[1:]:
            total = total + r[...].astype(f32)
        return total

    def own_half(length):
        half_length = length // 2
        return pl.ds(pl.multiple_of((lax.axis_index("ctx") & 1) * half_length, half_length), half_length)

    def own_piece(length):
        piece = length // (2 * n_batch)
        place = ((lax.axis_index("ctx") & 1) * n_batch + lax.axis_index("batch")) * piece
        return pl.ds(pl.multiple_of(place, piece), piece)

    up_piece = width // (2 * n_batch)
    down_piece = ff // (2 * n_batch)
    piece_rows = max(up_piece, down_piece)

    def pre_body(*refs):
        sources, (gate, up, down, wq, wo) = refs[:7], refs[7:12]
        normed_o, kv_o, unit_o, scale_o, cos_o, sin_o, idx_o, start_o, gate_o, piece_o, wq_o, wo_o = refs[12:24]
        col_pos, col_idx, sem = refs[24:27]
        table, hid, pos, gains, hgains, freqs, wkv = refs[27:]
        loads = [pltpu.make_async_copy(a, b, sem.at[i]) for i, (a, b) in enumerate(zip(sources, refs[27:]))]
        moves = [
            pltpu.make_async_copy(up.at[own_piece(width), :], piece_o.at[:up_piece, :ff], sem.at[7]),
            pltpu.make_async_copy(down.at[own_piece(ff), :], piece_o.at[:down_piece, ff:], sem.at[8]),
            pltpu.make_async_copy(gate.at[own_half(width), :], gate_o, sem.at[9]),
            pltpu.make_async_copy(wq, wq_o, sem.at[10]),
            pltpu.make_async_copy(wo, wo_o, sem.at[11]),
        ]
        for move in loads + moves:
            move.start()
        if up_piece < piece_rows:
            piece_o[up_piece:, :ff] = jnp.zeros((piece_rows - up_piece, ff), bf16)
        if down_piece < piece_rows:
            piece_o[down_piece:, ff:] = jnp.zeros((piece_rows - down_piece, width), bf16)
        for load in loads:
            load.wait()
        eye = lax.broadcasted_iota(jnp.int32, (block_len, block_len), 0) == lax.broadcasted_iota(
            jnp.int32, (block_len, block_len), 1
        )
        for j in range(blocks):
            t = table[lax.axis_index("ctx") * blocks + j]
            line = pos[:, pl.ds(pl.multiple_of(t * block_len, block_len), block_len)].astype(f32)
            column = jnp.sum(jnp.where(eye, line, 0.0), axis=1, keepdims=True)
            place = lax.broadcasted_iota(jnp.int32, (block_len, 1), 0) + t * block_len
            col_pos[j * block_len : (j + 1) * block_len, :] = column
            col_idx[j * block_len : (j + 1) * block_len, :] = place.astype(f32)
        for k in range(2):
            at = own_rows(k)
            x = hid[at, :].astype(f32)
            normed_o[part(k), :] = (x * rms_scale(x) * gains[0:1, :]).astype(bf16)
            p = col_pos[at, :]
            angle = p * freqs[...]
            cos_o[part(k), :] = jnp.cos(angle)
            sin_o[part(k), :] = jnp.sin(angle)
            idx_o[part(k), :] = col_idx[at, :]
            start_o[part(k), :] = col_idx[at, :] - p
        kv = product(normed_o[...], wkv[...])
        key = kv[:, :head_dim]
        scale = rms_scale(key)
        unit = key * scale
        unit_o[...] = unit
        scale_o[...] = scale
        kv_o[:, :head_dim] = rotate(unit * hgains[1:2, :], cos_o[...], sin_o[...]).astype(bf16)
        kv_o[:, head_dim:] = kv[:, head_dim:].astype(bf16)
        for move in moves:
            move.wait()

    sources = (block_table, hidden, positions, norm_gains, head_norm_gains, freq, key_value_weight)
    normed, kv_mine, unit_k, scale_k, cosine, sine, idx, start, gate_pack, piece_pack, wq_near, wo_near = kernel_call(
        pre_body,
        tuple(
            pltpu.with_memory_space_constraint(x, pltpu.HBM)
            for x in (*sources, gate_weight, up_weight, down_weight, query_weight, output_weight)
        ),
        [
            ((rows, width), bf16),
            ((rows, 2 * head_dim), bf16),
            ((rows, head_dim), f32),
            ((rows, 1), f32),
            ((rows, half), f32),
            ((rows, half), f32),
            ((rows, 1), f32),
            ((rows, 1), f32),
            ((width // 2, ff), bf16),
            ((piece_rows, ff + width), bf16),
            (query_weight.shape, bf16),
            (output_weight.shape, bf16),
        ],
        scratch=[pltpu.VMEM((rows, 1), f32), pltpu.VMEM((rows, 1), f32), pltpu.SemaphoreType.DMA((12,))]
        + [pltpu.SMEM(block_table.shape, block_table.dtype)]
        + [pltpu.VMEM(x.shape, x.dtype) for x in sources[1:]],
        in_hbm=12,
    )

    gate_near = neighbour(gate_pack)
    piece_near = neighbour(piece_pack)
    pieces = [piece_near] + [swap(piece_near, "batch", n_batch, k) for k in range(1, n_batch)]

    def stack_body(*refs):
        up_o, down_o = refs[n_batch:]
        for k in range(n_batch):
            b = lax.axis_index("batch") ^ k
            up_o[pl.ds(pl.multiple_of(b * up_piece, up_piece), up_piece), :] = refs[k][:up_piece, :ff]
            down_o[pl.ds(pl.multiple_of(b * down_piece, down_piece), down_piece), :] = refs[k][
                :down_piece, ff:
            ]

    up_near, down_near = kernel_call(stack_body, tuple(pieces), [((width // 2, ff), bf16), ((ff // 2, width), bf16)])

    def whole_body(*refs):
        for mine, far, whole in zip(refs[:3], refs[3:6], refs[6:]):
            length = mine.shape[0]
            for k, ref in enumerate((mine, far)):
                place = ((lax.axis_index("ctx") & 1) ^ k) * length
                whole[pl.ds(pl.multiple_of(place, length), length), :] = ref[...]

    halves = (gate_near, up_near, down_near)
    near_weights = kernel_call(
        whole_body,
        halves + tuple(other_core(h) for h in halves),
        [((width, ff), bf16), ((width, ff), bf16), ((ff, width), bf16)],
    )

    if paired:
        kvs = [kv_mine, other_core(kv_mine)]
    else:
        kvs = [lax.all_gather(kv_mine, "ctx", axis=0, tiled=True)]

    def query_body(nrm, wq, hgains, cos, sin, q_o, unit_o, scale_o):
        raw = product(nrm[...], wq[...])
        for h in range(heads):
            cols = slice(h * head_dim, (h + 1) * head_dim)
            scale = rms_scale(raw[:, cols])
            unit = raw[:, cols] * scale
            unit_o[:, cols] = unit
            scale_o[:, h : h + 1] = scale
            q_o[:, cols] = (rotate(unit * hgains[0:1, :], cos[...], sin[...]) * root).astype(bf16)

    queries, unit_q, scale_q = kernel_call(
        query_body,
        (normed, wq_near, head_norm_gains, cosine, sine),
        [((rows, q_width), bf16), ((rows, q_width), f32), ((rows, heads), f32)],
    )

    def attend_body(*refs):
        table, q, idx_r, start_r, wo = refs[:5]
        kv = refs[5 : 5 + len(kvs)]
        probs_o, context_o, mine_o, send_o = refs[5 + len(kvs) :]
        low = lax.axis_index("tp") & 1
        ctx = lax.axis_index("ctx")
        order = [ctx, ctx ^ 1] if paired else list(range(n_ctx))
        lane = lax.broadcasted_iota(jnp.int32, (1, seq), 1)
        key_idx = lane
        for m, rank in enumerate(order):
            for at in range(0, rows, unit_len):
                first = (low ^ (at // share)) * share + at % share
                base = table[rank * blocks + lax.div(first, block_len)] * block_len
                base = base + lax.rem(first, block_len)
                begin = m * rows + at
                key_idx = jnp.where(
                    (lane >= begin) & (lane < begin + unit_len), lane + (base - begin), key_idx
                )
        key_idx = key_idx.astype(f32)
        allowed = (key_idx <= idx_r[...]) & (key_idx >= start_r[...])
        length = seq // len(kvs)
        for h in range(heads):
            cols = slice(h * head_dim, (h + 1) * head_dim)
            scores = jnp.concatenate(
                [back_product(q[:, cols], r[:, :head_dim]) for r in kv], axis=1
            )
            scores = jnp.where(allowed, scores, -jnp.inf)
            top = jnp.max(scores, axis=1, keepdims=True)
            expo = jnp.exp(scores - top)
            inverse = 1.0 / jnp.sum(expo, axis=1, keepdims=True)
            probs_o[h] = expo * inverse
            probs = expo.astype(bf16)
            mixed = product(probs[:, :length], kv[0][:, head_dim:])
            for m in range(1, len(kvs)):
                mixed = mixed + product(probs[:, m * length : (m + 1) * length], kv[m][:, head_dim:])
            context_o[:, cols] = (mixed * inverse).astype(bf16)
        total = product(context_o[...], wo[...])
        mine_o[...] = total[part(0)]
        send_o[...] = total[part(1)].astype(bf16)

    probs, context, attn_mine, attn_send = kernel_call(
        attend_body,
        (block_table, queries, idx, start, wo_near, *kvs),
        [
            ((heads, rows, seq), f32),
            ((rows, q_width), bf16),
            ((share, width), f32),
            ((share, width), bf16),
        ],
        tables=1,
    )

    def meet_body(a, b, o):
        o[...] = (a[...] + b[...].astype(f32)).astype(bf16)

    def meet(mine, got):
        return kernel_call(meet_body, (mine, got), [((share, width), bf16)])[0]

    attn_met = meet(attn_mine, neighbour(attn_send))
    attn_terms = exchanged(attn_met)
    n_terms = len(attn_terms)
    weights = (gate_weight, up_weight, down_weight, *near_weights)

    def ff_groups(refs):
        return [
            (refs[0][...], refs[1][...], refs[2][...], slice(0, ff)),
            (refs[3][...], refs[4][...], refs[5][...], slice(ff, 2 * ff)),
        ]

    def with_earlier(value, earlier, out):
        for k, ref in enumerate(earlier):
            out[k * piece : (k + 1) * piece, :] = ref[...]
        out[len(earlier) * piece :, :] = value

    def feed(k, earlier):
        rows_k = slice(k * piece, (k + 1) * piece)
        full = (k + 1) * piece

        def feed_body(*refs):
            hid, gains = refs[:2]
            groups = ff_groups(refs[2:8])
            terms = refs[8 : 8 + n_terms]
            before = refs[8 + n_terms : 8 + n_terms + len(earlier)]
            unit_o, scale_o, mixed_o, x_o, act_o, near_o, gate_o, up_o, send_o = refs[8 + n_terms + len(earlier) :]
            attn = terms[0][rows_k, :].astype(f32)
            for r in terms[1:]:
                attn = attn + r[rows_k, :].astype(f32)
            scale = rms_scale(attn)
            unit = attn * scale
            mixed = hid[own_stream(k), :].astype(f32) + unit * gains[1:2, :]
            unit_o[...] = unit
            scale_o[...] = scale
            mixed_o[...] = mixed
            x = (mixed * rms_scale(mixed) * gains[2:3, :]).astype(bf16)
            x_o[...] = x
            total = None
            for at, (wg, wu, wd, cols) in enumerate(groups):
                gate = product(x, wg)
                up = product(x, wu)
                gate_o[:, cols] = gate
                up_o[:, cols] = up
                inner = gelu_coef * (gate + 0.044715 * gate * gate * gate)
                act = (0.5 * gate * (1.0 + jnp.tanh(inner)) * up).astype(bf16)
                term = product(act, wd)
                total = term if total is None else total + term
                if at == 0:
                    act_o[...] = act
                else:
                    with_earlier(act, before, near_o)
            send_o[...] = total.astype(bf16)

        return kernel_call(
            feed_body,
            (hidden, norm_gains, *weights, *attn_terms, *earlier),
            [
                ((piece, width), f32),
                ((piece, 1), f32),
                ((piece, width), f32),
                ((piece, width), bf16),
                ((piece, ff), bf16),
                ((full, ff), bf16),
                ((piece, 2 * ff), f32),
                ((piece, 2 * ff), f32),
                ((piece, width), bf16),
            ],
        )

    def slope_body(gate_r, up_r, gelu_o, slope_o):
        v = gate_r[...]
        inner = gelu_coef * (v + 0.044715 * v * v * v)
        tanh_val = jnp.tanh(inner)
        gelu_o[...] = 0.5 * v * (1.0 + tanh_val)
        slope = 0.5 * (1.0 + tanh_val) + 0.5 * v * (1.0 - tanh_val * tanh_val) * gelu_coef * (
            1.0 + 3.0 * 0.044715 * v * v
        )
        slope_o[...] = slope * up_r[...]

    fed, ff_terms, slopes = [], [], []
    act_send = []
    for k in range(streams):
        fed.append(feed(k, act_send))
        act_send = [fed[k][5]]
        ff_terms.append(exchanged(fed[k][8]))
        slopes.append(kernel_call(slope_body, tuple(fed[k][6:8]), [((piece, 2 * ff), f32)] * 2))
    act_near = neighbour(act_send[0])
    act_mine = [f[4] for f in fed]
    ff_in = [f[3] for f in fed]

    def feed_back(k, earlier):
        full = (k + 1) * piece

        def back_body(*refs):
            gains, mixed_r, cot_r, gelu_r, slope_r = refs[:5]
            groups = ff_groups(refs[5:11])
            ff_out = summed(refs[11 : 11 + n_terms])
            before = refs[11 + n_terms : 11 + n_terms + len(earlier)]
            hidden_o, gain_o, dout_o, dgate_o, dup_o, send_o = refs[11 + n_terms + len(earlier) :]
            scale = rms_scale(ff_out)
            unit = ff_out * scale
            with_earlier((mixed_r[...] + unit * gains[3:4, :]).astype(bf16), before[:1], hidden_o)
            grad = cot_r[own_stream(k), :].astype(f32)
            gain_o[...] = jnp.sum(grad * unit, axis=0, keepdims=True) * (1.0 / copies)
            d_out = rms_back(grad, unit, scale, gains[3:4, :]).astype(bf16)
            with_earlier(d_out, before[1:], dout_o)
            total = None
            for wg, wu, wd, cols in groups:
                d_act = back_product(d_out, wd)
                d_gate = (d_act * slope_r[:, cols]).astype(bf16)
                d_up = (d_act * gelu_r[:, cols]).astype(bf16)
                term = back_product(d_gate, wg) + back_product(d_up, wu)
                total = term if total is None else total + term
                dgate_o[:, cols] = d_gate
                dup_o[:, cols] = d_up
            send_o[...] = total.astype(bf16)

        return kernel_call(
            back_body,
            (norm_gains, fed[k][2], cot, *slopes[k], *weights, *ff_terms[k], *earlier),
            [
                ((full, width), bf16),
                ((1, width), f32),
                ((full, width), bf16),
                ((piece, 2 * ff), bf16),
                ((piece, 2 * ff), bf16),
                ((piece, width), bf16),
            ],
        )

    backed, dffin_terms = [], []
    earlier = ()
    for k in range(streams):
        backed.append(feed_back(k, earlier))
        earlier = (backed[k][0], backed[k][2])
        dffin_terms.append(exchanged(backed[k][5]))
    hidden_mine, d_ff_out = earlier
    gain_o = [r[1] for r in backed]
    d_gate = [r[3] for r in backed]
    d_up = [r[4] for r in backed]
    hidden_near = neighbour(hidden_mine)
    d_ff_near = neighbour(d_ff_out)

    def arrange(acc, outs):
        if not paired:
            outs[0][...] = acc[...]
            return
        batch = lax.axis_index("batch")
        ctx = lax.axis_index("ctx")
        for side in range(2):
            for k in range(n_batch):
                first = ((batch ^ k) * n_ctx + (ctx ^ side)) * out_rows
                outs[side][k * out_rows : (k + 1) * out_rows, :] = acc[
                    pl.ds(pl.multiple_of(first, out_rows), out_rows), :
                ].astype(bf16)

    def grad_call(fill, args, *columns):
        count = 2 if paired else 1

        def body(*refs):
            accs = refs[len(args) + count * len(columns) :]
            fill(*refs[: len(args)], *accs)
            for k, acc in enumerate(accs):
                at = len(args) + count * k
                arrange(acc, refs[at : at + count])

        outs = []
        for c in columns:
            outs += [((n_batch * out_rows, c), bf16)] * 2 if paired else [((width, c), f32)]
        terms = kernel_call(body, args, outs, scratch=[pltpu.VMEM((width, c), f32) for c in columns])
        return [terms[count * k : count * (k + 1)] for k in range(len(columns))]

    def reduce_grads(*grads):
        if not paired:
            sums = [
                lax.psum_scatter(g[0], ("batch", "ctx"), scatter_dimension=0, tiled=True) for g in grads
            ]
            return [jnp.concatenate(sums, axis=1)]
        columns = sum(g[0].shape[1] for g in grads)
        pairs = [x for keep, send in grads for x in (keep, other_core(send))]

        def add_body(*refs):
            at = 0
            for a, b in zip(refs[: len(pairs) : 2], refs[1 : len(pairs) : 2]):
                total = a[...].astype(f32) + b[...].astype(f32)
                cols = slice(at, at + total.shape[1])
                at = cols.stop
                for k, out in enumerate(refs[len(pairs) :]):
                    out[:, cols] = total[k * out_rows : (k + 1) * out_rows].astype(out.dtype)

        parts = kernel_call(
            add_body, tuple(pairs), [((out_rows, columns), f32)] + [((out_rows, columns), bf16)] * (n_batch - 1)
        )
        return [parts[0]] + [swap(parts[k], "batch", n_batch, k) for k in range(1, n_batch)]

    def ff_grad_fill(*refs):
        x, d_gate_v, d_up_v = (joined(refs[k * streams : (k + 1) * streams]) for k in range(3))
        near_acc, own_acc = refs[3 * streams :]
        for at, right in enumerate((d_gate_v, d_up_v)):
            total = lead_product(x, right)
            own_acc[:, at * ff : (at + 1) * ff] = total[:, :ff]
            near_acc[:, at * ff : (at + 1) * ff] = total[:, ff:]

    near_grads, own_grads = grad_call(ff_grad_fill, (*ff_in, *d_gate, *d_up), 2 * ff, 2 * ff)
    mid_terms = reduce_grads(near_grads)

    def mix_back(k):
        def mix_back_body(gains, mixed_r, unit_r, scale_r, cot_r, *refs):
            d_in = summed(refs[:n_terms])
            dmixed_o, dattn_o, gain_f_o, gain_a_o = refs[n_terms:]
            mixed_v = mixed_r[...]
            scale = rms_scale(mixed_v)
            unit_f = mixed_v * scale
            gain_f_o[...] = jnp.sum(d_in * unit_f, axis=0, keepdims=True) * (1.0 / copies)
            d_mix = cot_r[own_stream(k), :].astype(f32) + rms_back(d_in, unit_f, scale, gains[2:3, :])
            dmixed_o[...] = d_mix
            unit = unit_r[...]
            gain_a_o[...] = jnp.sum(d_mix * unit, axis=0, keepdims=True) * (1.0 / copies)
            dattn_o[...] = rms_back(d_mix, unit, scale_r[...], gains[1:2, :]).astype(bf16)

        terms = dffin_terms[k]
        if k == streams - 1:
            terms = [terms[0]] + [after(t, near_grads[0]) for t in terms[1:]]
        unit_a, scale_a, mixed = fed[k][:3]
        return kernel_call(
            mix_back_body,
            (norm_gains, mixed, unit_a, scale_a, cot, *terms),
            [((piece, width), f32), ((piece, width), bf16), ((1, width), f32), ((1, width), f32)],
        )

    mix_backs = [mix_back(k) for k in range(streams)]
    d_mixed = [m[0] for m in mix_backs]
    gain_f = [m[2] for m in mix_backs]
    gain_a = [m[3] for m in mix_backs]
    near_parts = [neighbour(m[1]) for m in mix_backs]
    near_parts[-1] = after(near_parts[-1], mid_terms[0])
    d_attn = (*(m[1] for m in mix_backs), *near_parts)

    def attend_back_body(*refs):
        wo, probs_r, q = refs[:3]
        kv = refs[3 : 3 + len(kvs)]
        at = 3 + len(kvs) + len(d_attn)
        d_out = joined(refs[3 + len(kvs) : at])
        dq_o = refs[at]
        dkv_o = refs[at + 1 :]
        d_context = back_product(d_out, wo[...]).astype(bf16)
        length = seq // len(kvs)
        for h in range(heads):
            cols = slice(h * head_dim, (h + 1) * head_dim)
            probs_v = probs_r[h]
            d_probs = jnp.concatenate(
                [back_product(d_context[:, cols], r[:, head_dim:]) for r in kv], axis=1
            )
            delta = jnp.sum(probs_v * d_probs, axis=1, keepdims=True)
            d_scores = (probs_v * (d_probs - delta)).astype(bf16)
            rounded = probs_v.astype(bf16)
            d_q = None
            for m, r in enumerate(kv):
                span = slice(m * length, (m + 1) * length)
                term = product(d_scores[:, span], r[:, :head_dim])
                d_q = term if d_q is None else d_q + term
                d_k = lead_product(d_scores[:, span], q[:, cols])
                d_v = lead_product(rounded[:, span], d_context[:, cols])
                if h > 0:
                    d_k = d_k + dkv_o[m][:, :head_dim].astype(f32)
                    d_v = d_v + dkv_o[m][:, head_dim:].astype(f32)
                dkv_o[m][:, :head_dim] = d_k.astype(dkv_o[m].dtype)
                dkv_o[m][:, head_dim:] = d_v.astype(dkv_o[m].dtype)
            dq_o[:, cols] = d_q

    if paired:
        dkv_outs = [((rows, 2 * head_dim), f32), ((rows, 2 * head_dim), f32 if heads > 1 else bf16)]
    else:
        dkv_outs = [((seq, 2 * head_dim), f32)]
    attended_back = kernel_call(
        attend_back_body, (wo_near, probs, queries, *kvs, *d_attn), [((rows, q_width), f32)] + dkv_outs
    )
    d_q = attended_back[0]
    if paired:
        dkv_terms = [attended_back[1], other_core(attended_back[2])]
    else:
        dkv_terms = [lax.psum_scatter(attended_back[1], "ctx", scatter_dimension=0, tiled=True)]

    def query_back_body(dq, unit_r, scale_r, cos, sin, hgains, wq, draw_o, dn_o, gain_o):
        gain = jnp.zeros((1, head_dim), f32)
        for h in range(heads):
            cols = slice(h * head_dim, (h + 1) * head_dim)
            d_unit = rotate_back(dq[:, cols], cos[...], sin[...]) * root
            unit = unit_r[:, cols]
            gain = gain + jnp.sum(d_unit * unit, axis=0, keepdims=True)
            draw_o[:, cols] = rms_back(d_unit, unit, scale_r[:, h : h + 1], hgains[0:1, :]).astype(bf16)
        gain_o[...] = gain
        dn_o[...] = back_product(draw_o[...], wq[...])

    d_query_raw, dn_query, gain_q = kernel_call(
        query_back_body,
        (d_q, unit_q, scale_q, cosine, sine, head_norm_gains, wq_near),
        [((rows, q_width), bf16), ((rows, width), f32), ((1, head_dim), f32)],
    )

    def pre_back_body(dn, unit_r, scale_r, cos, sin, hgains, wkv, *refs):
        count = len(dkv_terms)
        d_kv = summed(refs[:count])
        draw_o, gain_o, mine_o, send_o = refs[count:]
        d_unit = rotate_back(d_kv[:, :head_dim], cos[...], sin[...])
        unit = unit_r[...]
        gain_o[...] = jnp.sum(d_unit * unit, axis=0, keepdims=True)
        draw_o[:, :head_dim] = rms_back(d_unit, unit, scale_r[...], hgains[1:2, :]).astype(bf16)
        draw_o[:, head_dim:] = d_kv[:, head_dim:].astype(bf16)
        total = dn[...] + back_product(draw_o[...], wkv[...])
        mine_o[...] = total[part(0)]
        send_o[...] = total[part(1)].astype(bf16)

    d_kv_raw, gain_k, dn_mine, dn_send = kernel_call(
        pre_back_body,
        (dn_query, unit_k, scale_k, cosine, sine, head_norm_gains, key_value_weight, *dkv_terms),
        [
            ((rows, 2 * head_dim), bf16),
            ((1, head_dim), f32),
            ((share, width), f32),
            ((share, width), bf16),
        ],
    )
    dn_terms = exchanged(meet(dn_mine, neighbour(dn_send)))

    def mid_body(*refs):
        refs[-1][...] = summed(refs[:-1]).astype(bf16)

    (mid_send,) = kernel_call(mid_body, tuple(mid_terms), [((out_rows, 2 * ff), bf16)])
    mid_near = neighbour(mid_send)

    def down_grad_fill(*refs):
        refs[-1][...] = lead_product(joined(refs[:2]), joined(refs[2:-1]))

    def out_grad_fill(*refs):
        refs[-1][...] = lead_product(joined(refs[:-2]), refs[-2][...])

    side_terms = reduce_grads(
        own_grads,
        *grad_call(down_grad_fill, (d_ff_out, d_ff_near, *act_mine, act_near), ff),
        *grad_call(out_grad_fill, (*d_attn, context), q_width),
    )

    def side_body(*refs):
        total = summed(refs[: len(side_terms)])
        near, gate_o, up_o, down_o, out_o = refs[len(side_terms) :]
        gate_o[...] = total[:, :ff] + near[:, :ff].astype(f32)
        up_o[...] = total[:, ff : 2 * ff] + near[:, ff:].astype(f32)
        down_o[...] = total[:, 2 * ff : 3 * ff]
        out_o[...] = total[:, 3 * ff :]

    gate_grad, up_grad, down_grad, out_grad = kernel_call(
        side_body, (*side_terms, mid_near), [((out_rows, ff), f32)] * 3 + [((out_rows, q_width), f32)]
    )

    lanes = 128
    kv_at = q_width
    gain_at = q_width + 2 * head_dim

    def last_grad_fill(nrm, draw, dkv, hid, g_q, g_k, mine, send, *refs):
        acc = refs[-1]
        g_o, g_f, g_a = (summed(refs[k * streams : (k + 1) * streams]) for k in range(3))
        acc[:, :kv_at] = lead_product(nrm[...], draw[...])
        acc[:, kv_at:gain_at] = lead_product(nrm[...], dkv[...])
        g_in = jnp.zeros((1, width), f32)
        for k, terms in enumerate((mine, send)):
            x = hid[own_rows(k), :].astype(f32)
            g_in = g_in + jnp.sum(terms[...].astype(f32) * x * rms_scale(x), axis=0, keepdims=True)
        line = lax.broadcasted_iota(jnp.int32, (lanes, width), 0)
        packed = jnp.where(line == 0, g_in, 0.0)
        for at, row in enumerate((g_a, g_f, g_o), 1):
            packed = jnp.where(line == at, row, packed)
        acc[:, gain_at:] = packed.T
        line = lax.broadcasted_iota(jnp.int32, (lanes, head_dim), 0)
        packed = jnp.where(line == 4, g_q[...], jnp.where(line == 5, g_k[...], 0.0)).T
        for d in range(shards):
            at = slice(d * out_rows, d * out_rows + head_rows)
            acc[at, gain_at:] = acc[at, gain_at:] + packed[d * head_rows : (d + 1) * head_rows]

    last_terms = reduce_grads(
        *grad_call(
            last_grad_fill,
            (normed, d_query_raw, d_kv_raw, hidden, gain_q, gain_k, dn_mine, dn_send, *gain_o, *gain_f, *gain_a),
            gain_at + lanes,
        ),
    )

    def last_body(*refs):
        count = len(last_terms)
        total = summed(refs[:count])
        refs[count][...] = total[:, :kv_at]
        refs[count + 1][...] = total[:, kv_at:].astype(bf16)

    query_grad, kv_mine_sum = kernel_call(
        last_body, tuple(last_terms), [((out_rows, q_width), f32), ((out_rows, 2 * head_dim + lanes), bf16)]
    )
    kv_sums = [kv_mine_sum] + [swap(kv_mine_sum, "tp", n_tp, k) for k in range(1, n_tp)]

    def kv_body(*refs):
        terms = [r[...].astype(f32) for r in refs[:n_tp]]
        while len(terms) > 1:
            terms = [a + b for a, b in zip(terms[::2], terms[1::2])]
        refs[n_tp][...] = terms[0][:, : 2 * head_dim]
        lines = terms[0][:, 2 * head_dim :].T
        refs[n_tp + 1][...] = lines[:4]
        refs[n_tp + 2][...] = lines[4:6, :head_rows]

    kv_grad, gain_grad, head_gain_grad = kernel_call(
        kv_body, tuple(kv_sums), [((out_rows, 2 * head_dim), f32), ((4, out_rows), f32), ((2, head_rows), f32)]
    )

    def input_back_body(hid, gains, *refs):
        d_mix = joined(refs[:streams])
        d_normed = summed(refs[streams:-1])
        x = hid[own_rows(0), :].astype(f32)
        scale = rms_scale(x)
        refs[-1][...] = (d_mix + rms_back(d_normed, x * scale, scale, gains[0:1, :])).astype(bf16)

    (input_mine,) = kernel_call(input_back_body, (hidden, norm_gains, *d_mixed, *dn_terms), [((share, width), bf16)])

    def place_body(a, b, o):
        o[own_rows(0), :] = a[...]
        o[own_rows(1), :] = b[...]

    def placed(mine, near):
        (whole,) = kernel_call(place_body, (mine, near), [((rows, width), bf16)])
        return whole.reshape(hidden_in.shape)

    return (
        placed(hidden_mine, hidden_near),
        placed(input_mine, neighbour(input_mine)),
        query_grad,
        kv_grad,
        out_grad.T,
        gate_grad,
        up_grad,
        down_grad.T,
        gain_grad,
        head_gain_grad,
    )


def solution(mesh):
    return jax.shard_map(
        on_device,
        mesh=mesh,
        in_specs=(
            P("batch", "ctx", None, None),
            P("batch", None),
            P(),
            P(),
            P(),
            P(None, "tp"),
            P(),
            P("tp", None),
            P(None, "tp"),
            P(None, "tp"),
            P("tp", None),
            P("batch", "ctx", None, None),
        ),
        out_specs=(
            P("batch", "ctx", None, None),
            P("batch", "ctx", None, None),
            P(("batch", "ctx"), "tp"),
            P(("batch", "ctx"), None),
            P("tp", ("batch", "ctx")),
            P(("batch", "ctx"), "tp"),
            P(("batch", "ctx"), "tp"),
            P("tp", ("batch", "ctx")),
            P(None, ("batch", "ctx")),
            P(None, ("batch", "ctx")),
        ),
        check_vma=False,
    )
```

```python
import functools

import jax
import jax.numpy as jnp
import numpy as np
from jax import lax
from jax.experimental import pallas as pl
from jax.experimental.pallas import tpu as pltpu
from jax.sharding import PartitionSpec as P


epsilon = 1e-06
rope_base = 1000000.0
gelu_coef = 0.7978845608028654
f32 = jnp.float32
bf16 = jnp.bfloat16


def rms_scale(v):
    return lax.rsqrt(jnp.mean(v * v, axis=-1, keepdims=True) + epsilon)


def rms_back(grad, unit, scale, gain):
    weighted = grad * gain
    return scale * (weighted - unit * jnp.mean(unit * weighted, axis=-1, keepdims=True))


def rotate(v, cosine, sine):
    half = v.shape[-1] // 2
    first, second = (v[..., :half], v[..., half:])
    return jnp.concatenate(
        [first * cosine - second * sine, second * cosine + first * sine], axis=-1
    )


def rotate_back(g, cosine, sine):
    half = g.shape[-1] // 2
    first, second = (g[..., :half], g[..., half:])
    return jnp.concatenate(
        [first * cosine + second * sine, second * cosine - first * sine], axis=-1
    )


def product(left, right):
    return jnp.dot(left, right, preferred_element_type=f32)


def lead_product(left, right):
    return lax.dot_general(left, right, (((0,), (0,)), ((), ())), preferred_element_type=f32)


def back_product(left, right):
    return lax.dot_general(left, right, (((1,), (1,)), ((), ())), preferred_element_type=f32)


def kernel_call(body, args, outs, scratch=(), tables=0, in_hbm=0):
    moved = sum(a.size * a.dtype.itemsize for a in args)
    moved += sum(functools.reduce(lambda m, n: m * n, s, 1) * jnp.dtype(d).itemsize for s, d in outs)
    work = sum(
        functools.reduce(lambda m, n: m * n, s.shape, 1) * jnp.dtype(s.dtype).itemsize
        for s in scratch
        if s.dtype in (f32, bf16)
    )
    limit = min(60 << 20, (8 << 20) + 2 * (moved + work))
    return pl.pallas_call(
        body,
        out_shape=[jax.ShapeDtypeStruct(s, d) for s, d in outs],
        in_specs=[pl.BlockSpec(memory_space=pltpu.SMEM)] * tables
        + [pl.BlockSpec(memory_space=pltpu.VMEM)] * (len(args) - tables - in_hbm)
        + [pl.BlockSpec(memory_space=pltpu.HBM)] * in_hbm,
        out_specs=[pl.BlockSpec(memory_space=pltpu.VMEM)] * len(outs),
        scratch_shapes=list(scratch),
        cost_estimate=pl.CostEstimate(flops=0, bytes_accessed=moved, transcendentals=0),
        compiler_params=pltpu.CompilerParams(vmem_limit_bytes=limit),
    )(*args)


def swap(x, axis, size, k):
    return lax.ppermute(x, axis, [(i, i ^ k) for i in range(size)])


def after(x, *others):
    return lax.optimization_barrier((x, *others))[0]


def on_device(
    hidden_in,
    positions,
    block_table,
    norm_gains,
    head_norm_gains,
    query_weight,
    key_value_weight,
    output_weight,
    gate_weight,
    up_weight,
    down_weight,
    out_cotangent,
):
    n_tp = lax.axis_size("tp")
    n_ctx = lax.axis_size("ctx")
    n_batch = lax.axis_size("batch")
    blocks, block_len, width = hidden_in.shape[1:]
    rows = blocks * block_len
    head_dim = key_value_weight.shape[1] // 2
    half = head_dim // 2
    heads = query_weight.shape[1] // head_dim
    q_width = heads * head_dim
    ff = gate_weight.shape[1]
    seq = positions.shape[1]
    root = head_dim ** (-0.5)
    share = rows // 2
    streams = 2
    piece = share // streams
    unit_len = min(share, block_len)
    peers = tuple(range(2, n_tp, 2))
    copies = n_tp // 2
    shards = n_batch * n_ctx
    out_rows = width // shards
    head_rows = head_dim // shards
    paired = n_ctx == 2 and n_batch in (2, 4)

    hidden = hidden_in.reshape(rows, width)
    cot = out_cotangent.reshape(rows, width)
    freq = jnp.asarray(rope_base ** (-np.arange(half) * 2.0 / head_dim), f32).reshape(1, half)

    def part(k):
        return slice(k * share, (k + 1) * share)

    def own_rows(k):
        return pl.ds(pl.multiple_of(((lax.axis_index("tp") & 1) ^ k) * share, share), share)

    def own_stream(k):
        place = (lax.axis_index("tp") & 1) * share + k * piece
        return pl.ds(pl.multiple_of(place, piece), piece)

    def neighbour(x):
        return swap(x, "tp", n_tp, 1)

    def other_core(x):
        return swap(x, "ctx", n_ctx, 1)

    def exchanged(x):
        return [x] + [swap(x, "tp", n_tp, k) for k in peers]

    def joined(refs, columns=slice(None)):
        return jnp.concatenate([r[:, columns] for r in refs], axis=0)

    def summed(refs):
        total = refs[0][...].astype(f32)
        for r in refs[1:]:
            total = total + r[...].astype(f32)
        return total

    def own_half(length):
        half_length = length // 2
        return pl.ds(pl.multiple_of((lax.axis_index("ctx") & 1) * half_length, half_length), half_length)

    def own_piece(length):
        piece = length // (2 * n_batch)
        place = ((lax.axis_index("ctx") & 1) * n_batch + lax.axis_index("batch")) * piece
        return pl.ds(pl.multiple_of(place, piece), piece)

    up_piece = width // (2 * n_batch)
    down_piece = ff // (2 * n_batch)
    piece_rows = max(up_piece, down_piece)

    def pre_body(*refs):
        sources, (gate, up, down, wq, wo) = refs[:7], refs[7:12]
        normed_o, kv_o, unit_o, scale_o, cos_o, sin_o, idx_o, start_o, gate_o, piece_o, wq_o, wo_o = refs[12:24]
        key_o, hid, gains, hgains, wkv = refs[24:29]
        col_pos, col_idx, sem, table, pos, freqs = refs[29:]
        places = (table, hid, pos, gains, hgains, freqs, wkv)
        loads = [pltpu.make_async_copy(a, b, sem.at[i]) for i, (a, b) in enumerate(zip(sources, places))]
        moves = [
            pltpu.make_async_copy(up.at[own_piece(width), :], piece_o.at[:up_piece, :ff], sem.at[7]),
            pltpu.make_async_copy(down.at[own_piece(ff), :], piece_o.at[:down_piece, ff:], sem.at[8]),
            pltpu.make_async_copy(gate.at[own_half(width), :], gate_o, sem.at[9]),
            pltpu.make_async_copy(wq, wq_o, sem.at[10]),
            pltpu.make_async_copy(wo, wo_o, sem.at[11]),
        ]
        for move in loads + moves:
            move.start()
        if up_piece < piece_rows:
            piece_o[up_piece:, :ff] = jnp.zeros((piece_rows - up_piece, ff), bf16)
        if down_piece < piece_rows:
            piece_o[down_piece:, ff:] = jnp.zeros((piece_rows - down_piece, width), bf16)
        for load in loads:
            load.wait()
        eye = lax.broadcasted_iota(jnp.int32, (block_len, block_len), 0) == lax.broadcasted_iota(
            jnp.int32, (block_len, block_len), 1
        )
        for j in range(blocks):
            t = table[lax.axis_index("ctx") * blocks + j]
            line = pos[:, pl.ds(pl.multiple_of(t * block_len, block_len), block_len)].astype(f32)
            column = jnp.sum(jnp.where(eye, line, 0.0), axis=1, keepdims=True)
            place = lax.broadcasted_iota(jnp.int32, (block_len, 1), 0) + t * block_len
            col_pos[j * block_len : (j + 1) * block_len, :] = column
            col_idx[j * block_len : (j + 1) * block_len, :] = place.astype(f32)
        for k in range(2):
            at = own_rows(k)
            x = hid[at, :].astype(f32)
            normed_o[part(k), :] = (x * rms_scale(x) * gains[0:1, :]).astype(bf16)
            p = col_pos[at, :]
            angle = p * freqs[...]
            cos_o[part(k), :] = jnp.cos(angle)
            sin_o[part(k), :] = jnp.sin(angle)
            idx_o[part(k), :] = col_idx[at, :]
            start_o[part(k), :] = col_idx[at, :] - p
        kv = product(normed_o[...], wkv[...])
        key = kv[:, :head_dim]
        scale = rms_scale(key)
        unit = key * scale
        unit_o[...] = unit
        scale_o[...] = scale
        kv_o[:, :head_dim] = rotate(unit * hgains[1:2, :], cos_o[...], sin_o[...]).astype(bf16)
        kv_o[:, head_dim:] = kv[:, head_dim:].astype(bf16)
        low = lax.axis_index("tp") & 1
        ctx = lax.axis_index("ctx")
        order = [ctx, ctx ^ 1] if paired else list(range(n_ctx))
        lane = lax.broadcasted_iota(jnp.int32, (1, seq), 1)
        key_idx = lane
        for m, rank in enumerate(order):
            for at in range(0, rows, unit_len):
                first = (low ^ (at // share)) * share + at % share
                base = table[rank * blocks + lax.div(first, block_len)] * block_len
                base = base + lax.rem(first, block_len)
                begin = m * rows + at
                key_idx = jnp.where(
                    (lane >= begin) & (lane < begin + unit_len), lane + (base - begin), key_idx
                )
        key_o[...] = key_idx.astype(f32)
        for move in moves:
            move.wait()

    sources = (block_table, hidden, positions, norm_gains, head_norm_gains, freq, key_value_weight)
    first = kernel_call(
        pre_body,
        tuple(
            pltpu.with_memory_space_constraint(x, pltpu.HBM)
            for x in (*sources, gate_weight, up_weight, down_weight, query_weight, output_weight)
        ),
        [
            ((rows, width), bf16),
            ((rows, 2 * head_dim), bf16),
            ((rows, head_dim), f32),
            ((rows, 1), f32),
            ((rows, half), f32),
            ((rows, half), f32),
            ((rows, 1), f32),
            ((rows, 1), f32),
            ((width // 2, ff), bf16),
            ((piece_rows, ff + width), bf16),
            (query_weight.shape, bf16),
            (output_weight.shape, bf16),
            ((1, seq), f32),
        ]
        + [(x.shape, x.dtype) for x in (hidden, norm_gains, head_norm_gains, key_value_weight)],
        scratch=[
            pltpu.VMEM((rows, 1), f32),
            pltpu.VMEM((rows, 1), f32),
            pltpu.SemaphoreType.DMA((12,)),
            pltpu.SMEM(block_table.shape, block_table.dtype),
            pltpu.VMEM(positions.shape, positions.dtype),
            pltpu.VMEM(freq.shape, freq.dtype),
        ],
        in_hbm=12,
    )
    normed, kv_mine, unit_k, scale_k, cosine, sine, idx, start, gate_pack, piece_pack = first[:10]
    wq_near, wo_near, key_places, hidden, norm_gains, head_norm_gains, key_value_weight = first[10:]

    if paired:
        kvs = [kv_mine, other_core(kv_mine)]
    else:
        kvs = [lax.all_gather(kv_mine, "ctx", axis=0, tiled=True)]


    gate_near = neighbour(gate_pack)
    piece_near = neighbour(piece_pack)
    pieces = [piece_near] + [swap(piece_near, "batch", n_batch, k) for k in range(1, n_batch)]

    def stack_body(*refs):
        up_o, down_o = refs[n_batch:]
        for k in range(n_batch):
            b = lax.axis_index("batch") ^ k
            up_o[pl.ds(pl.multiple_of(b * up_piece, up_piece), up_piece), :] = refs[k][:up_piece, :ff]
            down_o[pl.ds(pl.multiple_of(b * down_piece, down_piece), down_piece), :] = refs[k][
                :down_piece, ff:
            ]

    up_near, down_near = kernel_call(stack_body, tuple(pieces), [((width // 2, ff), bf16), ((ff // 2, width), bf16)])

    def whole_body(*refs):
        for mine, far, whole in zip(refs[:3], refs[3:6], refs[6:]):
            length = mine.shape[0]
            for k, ref in enumerate((mine, far)):
                place = ((lax.axis_index("ctx") & 1) ^ k) * length
                whole[pl.ds(pl.multiple_of(place, length), length), :] = ref[...]

    halves = (gate_near, up_near, down_near)
    near_weights = kernel_call(
        whole_body,
        halves + tuple(other_core(h) for h in halves),
        [((width, ff), bf16), ((width, ff), bf16), ((ff, width), bf16)],
    )

    def query_body(nrm, wq, hgains, cos, sin, q_o, unit_o, scale_o):
        raw = product(nrm[...], wq[...])
        for h in range(heads):
            cols = slice(h * head_dim, (h + 1) * head_dim)
            scale = rms_scale(raw[:, cols])
            unit = raw[:, cols] * scale
            unit_o[:, cols] = unit
            scale_o[:, h : h + 1] = scale
            q_o[:, cols] = (rotate(unit * hgains[0:1, :], cos[...], sin[...]) * root).astype(bf16)

    queries, unit_q, scale_q = kernel_call(
        query_body,
        (normed, wq_near, head_norm_gains, cosine, sine),
        [((rows, q_width), bf16), ((rows, q_width), f32), ((rows, heads), f32)],
    )

    def attend_body(*refs):
        key_r, q, idx_r, start_r, wo = refs[:5]
        kv = refs[5 : 5 + len(kvs)]
        probs_o, context_o, mine_o, send_o = refs[5 + len(kvs) :]
        allowed = (key_r[...] <= idx_r[...]) & (key_r[...] >= start_r[...])
        length = seq // len(kvs)
        for h in range(heads):
            cols = slice(h * head_dim, (h + 1) * head_dim)
            scores = jnp.concatenate(
                [back_product(q[:, cols], r[:, :head_dim]) for r in kv], axis=1
            )
            scores = jnp.where(allowed, scores, -jnp.inf)
            top = jnp.max(scores, axis=1, keepdims=True)
            expo = jnp.exp(scores - top)
            inverse = 1.0 / jnp.sum(expo, axis=1, keepdims=True)
            probs_o[h] = expo * inverse
            probs = expo.astype(bf16)
            mixed = product(probs[:, :length], kv[0][:, head_dim:])
            for m in range(1, len(kvs)):
                mixed = mixed + product(probs[:, m * length : (m + 1) * length], kv[m][:, head_dim:])
            context_o[:, cols] = (mixed * inverse).astype(bf16)
        total = product(context_o[...], wo[...])
        mine_o[...] = total[part(0)]
        send_o[...] = total[part(1)].astype(bf16)

    probs, context, attn_mine, attn_send = kernel_call(
        attend_body,
        (key_places, queries, idx, start, wo_near, *kvs),
        [
            ((heads, rows, seq), f32),
            ((rows, q_width), bf16),
            ((share, width), f32),
            ((share, width), bf16),
        ],
    )

    def meet_body(a, b, o):
        o[...] = (a[...] + b[...].astype(f32)).astype(bf16)

    def meet(mine, got):
        return kernel_call(meet_body, (mine, got), [((share, width), bf16)])[0]

    attn_met = meet(attn_mine, neighbour(attn_send))
    attn_terms = exchanged(attn_met)
    n_terms = len(attn_terms)
    weights = (gate_weight, up_weight, down_weight, *near_weights)

    def ff_groups(refs):
        return [
            (refs[0][...], refs[1][...], refs[2][...], slice(0, ff)),
            (refs[3][...], refs[4][...], refs[5][...], slice(ff, 2 * ff)),
        ]

    def with_earlier(value, earlier, out):
        for k, ref in enumerate(earlier):
            out[k * piece : (k + 1) * piece, :] = ref[...]
        out[len(earlier) * piece :, :] = value

    def feed(k, earlier):
        rows_k = slice(k * piece, (k + 1) * piece)
        full = (k + 1) * piece

        def feed_body(*refs):
            hid, gains = refs[:2]
            groups = ff_groups(refs[2:8])
            terms = refs[8 : 8 + n_terms]
            before = refs[8 + n_terms : 8 + n_terms + len(earlier)]
            unit_o, scale_o, mixed_o, x_o, act_o, near_o, gate_o, up_o, send_o = refs[8 + n_terms + len(earlier) :]
            attn = terms[0][rows_k, :].astype(f32)
            for r in terms[1:]:
                attn = attn + r[rows_k, :].astype(f32)
            scale = rms_scale(attn)
            unit = attn * scale
            mixed = hid[own_stream(k), :].astype(f32) + unit * gains[1:2, :]
            unit_o[...] = unit
            scale_o[...] = scale
            mixed_o[...] = mixed
            x = (mixed * rms_scale(mixed) * gains[2:3, :]).astype(bf16)
            x_o[...] = x
            total = None
            for at, (wg, wu, wd, cols) in enumerate(groups):
                gate = product(x, wg)
                up = product(x, wu)
                gate_o[:, cols] = gate
                up_o[:, cols] = up
                inner = gelu_coef * (gate + 0.044715 * gate * gate * gate)
                act = (0.5 * gate * (1.0 + jnp.tanh(inner)) * up).astype(bf16)
                term = product(act, wd)
                total = term if total is None else total + term
                if at == 0:
                    act_o[...] = act
                else:
                    with_earlier(act, before, near_o)
            send_o[...] = total.astype(bf16)

        return kernel_call(
            feed_body,
            (hidden, norm_gains, *weights, *attn_terms, *earlier),
            [
                ((piece, width), f32),
                ((piece, 1), f32),
                ((piece, width), f32),
                ((piece, width), bf16),
                ((piece, ff), bf16),
                ((full, ff), bf16),
                ((piece, 2 * ff), f32),
                ((piece, 2 * ff), f32),
                ((piece, width), bf16),
            ],
        )

    def slope_body(gate_r, up_r, gelu_o, slope_o):
        v = gate_r[...]
        inner = gelu_coef * (v + 0.044715 * v * v * v)
        tanh_val = jnp.tanh(inner)
        gelu_o[...] = 0.5 * v * (1.0 + tanh_val)
        slope = 0.5 * (1.0 + tanh_val) + 0.5 * v * (1.0 - tanh_val * tanh_val) * gelu_coef * (
            1.0 + 3.0 * 0.044715 * v * v
        )
        slope_o[...] = slope * up_r[...]

    fed, ff_terms, slopes = [], [], []
    act_send = []
    for k in range(streams):
        fed.append(feed(k, act_send))
        act_send = [fed[k][5]]
        ff_terms.append(exchanged(fed[k][8]))
        slopes.append(kernel_call(slope_body, tuple(fed[k][6:8]), [((piece, 2 * ff), f32)] * 2))
    act_near = neighbour(act_send[0])
    act_mine = [f[4] for f in fed]
    ff_in = [f[3] for f in fed]

    def feed_back(k, earlier):
        full = (k + 1) * piece

        def back_body(*refs):
            gains, mixed_r, cot_r, gelu_r, slope_r = refs[:5]
            groups = ff_groups(refs[5:11])
            ff_out = summed(refs[11 : 11 + n_terms])
            before = refs[11 + n_terms : 11 + n_terms + len(earlier)]
            hidden_o, gain_o, dout_o, dgate_o, dup_o, send_o = refs[11 + n_terms + len(earlier) :]
            scale = rms_scale(ff_out)
            unit = ff_out * scale
            with_earlier((mixed_r[...] + unit * gains[3:4, :]).astype(bf16), before[:1], hidden_o)
            grad = cot_r[own_stream(k), :].astype(f32)
            gain_o[...] = jnp.sum(grad * unit, axis=0, keepdims=True) * (1.0 / copies)
            d_out = rms_back(grad, unit, scale, gains[3:4, :]).astype(bf16)
            with_earlier(d_out, before[1:], dout_o)
            total = None
            for wg, wu, wd, cols in groups:
                d_act = back_product(d_out, wd)
                d_gate = (d_act * slope_r[:, cols]).astype(bf16)
                d_up = (d_act * gelu_r[:, cols]).astype(bf16)
                term = back_product(d_gate, wg) + back_product(d_up, wu)
                total = term if total is None else total + term
                dgate_o[:, cols] = d_gate
                dup_o[:, cols] = d_up
            send_o[...] = total.astype(bf16)

        return kernel_call(
            back_body,
            (norm_gains, fed[k][2], cot, *slopes[k], *weights, *ff_terms[k], *earlier),
            [
                ((full, width), bf16),
                ((1, width), f32),
                ((full, width), bf16),
                ((piece, 2 * ff), bf16),
                ((piece, 2 * ff), bf16),
                ((piece, width), bf16),
            ],
        )

    backed, dffin_terms = [], []
    earlier = ()
    for k in range(streams):
        backed.append(feed_back(k, earlier))
        earlier = (backed[k][0], backed[k][2])
        dffin_terms.append(exchanged(backed[k][5]))
    hidden_mine, d_ff_out = earlier
    gain_o = [r[1] for r in backed]
    d_gate = [r[3] for r in backed]
    d_up = [r[4] for r in backed]
    hidden_near = neighbour(hidden_mine)
    d_ff_near = neighbour(d_ff_out)

    def arrange(acc, outs):
        if not paired:
            outs[0][...] = acc[...]
            return
        batch = lax.axis_index("batch")
        ctx = lax.axis_index("ctx")
        for side in range(2):
            for k in range(n_batch):
                first = ((batch ^ k) * n_ctx + (ctx ^ side)) * out_rows
                outs[side][k * out_rows : (k + 1) * out_rows, :] = acc[
                    pl.ds(pl.multiple_of(first, out_rows), out_rows), :
                ].astype(bf16)

    def grad_call(fill, args, *columns):
        count = 2 if paired else 1

        def body(*refs):
            accs = refs[len(args) + count * len(columns) :]
            fill(*refs[: len(args)], *accs)
            for k, acc in enumerate(accs):
                at = len(args) + count * k
                arrange(acc, refs[at : at + count])

        outs = []
        for c in columns:
            outs += [((n_batch * out_rows, c), bf16)] * 2 if paired else [((width, c), f32)]
        terms = kernel_call(body, args, outs, scratch=[pltpu.VMEM((width, c), f32) for c in columns])
        return [terms[count * k : count * (k + 1)] for k in range(len(columns))]

    def reduce_grads(*grads):
        if not paired:
            sums = [
                lax.psum_scatter(g[0], ("batch", "ctx"), scatter_dimension=0, tiled=True) for g in grads
            ]
            return [jnp.concatenate(sums, axis=1)]
        columns = sum(g[0].shape[1] for g in grads)
        pairs = [x for keep, send in grads for x in (keep, other_core(send))]

        def add_body(*refs):
            at = 0
            for a, b in zip(refs[: len(pairs) : 2], refs[1 : len(pairs) : 2]):
                total = a[...].astype(f32) + b[...].astype(f32)
                cols = slice(at, at + total.shape[1])
                at = cols.stop
                for k, out in enumerate(refs[len(pairs) :]):
                    out[:, cols] = total[k * out_rows : (k + 1) * out_rows].astype(out.dtype)

        parts = kernel_call(
            add_body, tuple(pairs), [((out_rows, columns), f32)] + [((out_rows, columns), bf16)] * (n_batch - 1)
        )
        return [parts[0]] + [swap(parts[k], "batch", n_batch, k) for k in range(1, n_batch)]

    def ff_grad_fill(*refs):
        x, d_gate_v, d_up_v = (joined(refs[k * streams : (k + 1) * streams]) for k in range(3))
        near_acc, own_acc = refs[3 * streams :]
        total = lead_product(x, d_gate_v)
        near_acc[:, :ff] = total[:, ff:]
        near_acc[:, 2 * ff :] = total[:, :ff]
        total = lead_product(x, d_up_v)
        near_acc[:, ff : 2 * ff] = total[:, ff:]
        own_acc[...] = total[:, :ff]

    near_grads, own_grads = grad_call(ff_grad_fill, (*ff_in, *d_gate, *d_up), 3 * ff, ff)
    mid_terms = reduce_grads(near_grads)

    def mix_back(k):
        def mix_back_body(gains, mixed_r, unit_r, scale_r, cot_r, *refs):
            d_in = summed(refs[:n_terms])
            dmixed_o, dattn_o, gain_f_o, gain_a_o = refs[n_terms:]
            mixed_v = mixed_r[...]
            scale = rms_scale(mixed_v)
            unit_f = mixed_v * scale
            gain_f_o[...] = jnp.sum(d_in * unit_f, axis=0, keepdims=True) * (1.0 / copies)
            d_mix = cot_r[own_stream(k), :].astype(f32) + rms_back(d_in, unit_f, scale, gains[2:3, :])
            dmixed_o[...] = d_mix
            unit = unit_r[...]
            gain_a_o[...] = jnp.sum(d_mix * unit, axis=0, keepdims=True) * (1.0 / copies)
            dattn_o[...] = rms_back(d_mix, unit, scale_r[...], gains[1:2, :]).astype(bf16)

        terms = dffin_terms[k]
        if k == streams - 1:
            terms = [terms[0]] + [after(t, near_grads[0]) for t in terms[1:]]
        unit_a, scale_a, mixed = fed[k][:3]
        return kernel_call(
            mix_back_body,
            (norm_gains, mixed, unit_a, scale_a, cot, *terms),
            [((piece, width), f32), ((piece, width), bf16), ((1, width), f32), ((1, width), f32)],
        )

    mix_backs = [mix_back(k) for k in range(streams)]
    d_mixed = [m[0] for m in mix_backs]
    gain_f = [m[2] for m in mix_backs]
    gain_a = [m[3] for m in mix_backs]
    near_parts = [neighbour(m[1]) for m in mix_backs]
    near_parts[-1] = after(near_parts[-1], mid_terms[0])
    d_attn = (*(m[1] for m in mix_backs), *near_parts)

    def attend_back_body(*refs):
        wo, probs_r, q = refs[:3]
        kv = refs[3 : 3 + len(kvs)]
        at = 3 + len(kvs) + len(d_attn)
        d_out = joined(refs[3 + len(kvs) : at])
        dq_o = refs[at]
        dkv_o = refs[at + 1 :]
        d_context = back_product(d_out, wo[...]).astype(bf16)
        length = seq // len(kvs)
        for h in range(heads):
            cols = slice(h * head_dim, (h + 1) * head_dim)
            probs_v = probs_r[h]
            d_probs = jnp.concatenate(
                [back_product(d_context[:, cols], r[:, head_dim:]) for r in kv], axis=1
            )
            delta = jnp.sum(probs_v * d_probs, axis=1, keepdims=True)
            d_scores = (probs_v * (d_probs - delta)).astype(bf16)
            rounded = probs_v.astype(bf16)
            d_q = None
            for m, r in enumerate(kv):
                span = slice(m * length, (m + 1) * length)
                term = product(d_scores[:, span], r[:, :head_dim])
                d_q = term if d_q is None else d_q + term
                d_k = lead_product(d_scores[:, span], q[:, cols])
                d_v = lead_product(rounded[:, span], d_context[:, cols])
                if h > 0:
                    d_k = d_k + dkv_o[m][:, :head_dim].astype(f32)
                    d_v = d_v + dkv_o[m][:, head_dim:].astype(f32)
                dkv_o[m][:, :head_dim] = d_k.astype(dkv_o[m].dtype)
                dkv_o[m][:, head_dim:] = d_v.astype(dkv_o[m].dtype)
            dq_o[:, cols] = d_q

    if paired:
        dkv_outs = [((rows, 2 * head_dim), f32), ((rows, 2 * head_dim), f32 if heads > 1 else bf16)]
    else:
        dkv_outs = [((seq, 2 * head_dim), f32)]
    attended_back = kernel_call(
        attend_back_body, (wo_near, probs, queries, *kvs, *d_attn), [((rows, q_width), f32)] + dkv_outs
    )
    d_q = attended_back[0]
    if paired:
        dkv_terms = [attended_back[1], other_core(attended_back[2])]
    else:
        dkv_terms = [lax.psum_scatter(attended_back[1], "ctx", scatter_dimension=0, tiled=True)]

    def query_back_body(dq, unit_r, scale_r, cos, sin, hgains, wq, draw_o, dn_o, gain_o):
        gain = jnp.zeros((1, head_dim), f32)
        for h in range(heads):
            cols = slice(h * head_dim, (h + 1) * head_dim)
            d_unit = rotate_back(dq[:, cols], cos[...], sin[...]) * root
            unit = unit_r[:, cols]
            gain = gain + jnp.sum(d_unit * unit, axis=0, keepdims=True)
            draw_o[:, cols] = rms_back(d_unit, unit, scale_r[:, h : h + 1], hgains[0:1, :]).astype(bf16)
        gain_o[...] = gain
        dn_o[...] = back_product(draw_o[...], wq[...])

    d_query_raw, dn_query, gain_q = kernel_call(
        query_back_body,
        (d_q, unit_q, scale_q, cosine, sine, head_norm_gains, wq_near),
        [((rows, q_width), bf16), ((rows, width), f32), ((1, head_dim), f32)],
    )

    def pre_back_body(dn, unit_r, scale_r, cos, sin, hgains, wkv, *refs):
        count = len(dkv_terms)
        d_kv = summed(refs[:count])
        draw_o, gain_o, mine_o, send_o = refs[count:]
        d_unit = rotate_back(d_kv[:, :head_dim], cos[...], sin[...])
        unit = unit_r[...]
        gain_o[...] = jnp.sum(d_unit * unit, axis=0, keepdims=True)
        draw_o[:, :head_dim] = rms_back(d_unit, unit, scale_r[...], hgains[1:2, :]).astype(bf16)
        draw_o[:, head_dim:] = d_kv[:, head_dim:].astype(bf16)
        total = dn[...] + back_product(draw_o[...], wkv[...])
        mine_o[...] = total[part(0)]
        send_o[...] = total[part(1)].astype(bf16)

    d_kv_raw, gain_k, dn_mine, dn_send = kernel_call(
        pre_back_body,
        (dn_query, unit_k, scale_k, cosine, sine, head_norm_gains, key_value_weight, *dkv_terms),
        [
            ((rows, 2 * head_dim), bf16),
            ((1, head_dim), f32),
            ((share, width), f32),
            ((share, width), bf16),
        ],
    )
    dn_terms = exchanged(meet(dn_mine, neighbour(dn_send)))

    def mid_body(*refs):
        total = summed(refs[:-2])
        refs[-2][...] = total[:, : 2 * ff].astype(bf16)
        refs[-1][...] = total[:, 2 * ff :]

    mid_send, mid_gate = kernel_call(mid_body, tuple(mid_terms), [((out_rows, 2 * ff), bf16), ((out_rows, ff), f32)])
    mid_near = neighbour(mid_send)

    def down_grad_fill(*refs):
        refs[-1][...] = lead_product(joined(refs[:2]), joined(refs[2:-1]))

    def out_grad_fill(*refs):
        refs[-1][...] = lead_product(joined(refs[:-2]), refs[-2][...])

    side_terms = reduce_grads(
        own_grads,
        *grad_call(down_grad_fill, (d_ff_out, d_ff_near, *act_mine, act_near), ff),
        *grad_call(out_grad_fill, (*d_attn, context), q_width),
    )

    def side_body(*refs):
        total = summed(refs[: len(side_terms)])
        mine, near, gate_o, up_o, down_o, out_o = refs[len(side_terms) :]
        gate_o[...] = mine[...] + near[:, :ff].astype(f32)
        up_o[...] = total[:, :ff] + near[:, ff:].astype(f32)
        down_o[...] = total[:, ff : 2 * ff]
        out_o[...] = total[:, 2 * ff :]

    gate_grad, up_grad, down_grad, out_grad = kernel_call(
        side_body, (*side_terms, mid_gate, mid_near), [((out_rows, ff), f32)] * 3 + [((out_rows, q_width), f32)]
    )

    lanes = 128
    kv_at = q_width
    gain_at = q_width + 2 * head_dim

    def last_grad_fill(nrm, draw, dkv, hid, g_q, g_k, mine, send, *refs):
        acc = refs[-1]
        g_o, g_f, g_a = (summed(refs[k * streams : (k + 1) * streams]) for k in range(3))
        acc[:, :kv_at] = lead_product(nrm[...], draw[...])
        acc[:, kv_at:gain_at] = lead_product(nrm[...], dkv[...])
        g_in = jnp.zeros((1, width), f32)
        for k, terms in enumerate((mine, send)):
            x = hid[own_rows(k), :].astype(f32)
            g_in = g_in + jnp.sum(terms[...].astype(f32) * x * rms_scale(x), axis=0, keepdims=True)
        line = lax.broadcasted_iota(jnp.int32, (lanes, width), 0)
        packed = jnp.where(line == 0, g_in, 0.0)
        for at, row in enumerate((g_a, g_f, g_o), 1):
            packed = jnp.where(line == at, row, packed)
        acc[:, gain_at:] = packed.T
        line = lax.broadcasted_iota(jnp.int32, (lanes, head_dim), 0)
        packed = jnp.where(line == 4, g_q[...], jnp.where(line == 5, g_k[...], 0.0)).T
        for d in range(shards):
            at = slice(d * out_rows, d * out_rows + head_rows)
            acc[at, gain_at:] = acc[at, gain_at:] + packed[d * head_rows : (d + 1) * head_rows]

    last_terms = reduce_grads(
        *grad_call(
            last_grad_fill,
            (normed, d_query_raw, d_kv_raw, hidden, gain_q, gain_k, dn_mine, dn_send, *gain_o, *gain_f, *gain_a),
            gain_at + lanes,
        ),
    )

    def last_body(*refs):
        count = len(last_terms)
        total = summed(refs[:count])
        refs[count][...] = total[:, :kv_at]
        refs[count + 1][...] = total[:, kv_at:].astype(bf16)

    query_grad, kv_mine_sum = kernel_call(
        last_body, tuple(last_terms), [((out_rows, q_width), f32), ((out_rows, 2 * head_dim + lanes), bf16)]
    )

    def pair_body(a, b, o):
        o[...] = (a[...].astype(f32) + b[...].astype(f32)).astype(bf16)

    def kv_body(a, b, kv_o, gain_o, head_o):
        total = a[...].astype(f32) + b[...].astype(f32)
        kv_o[...] = total[:, : 2 * head_dim]
        lines = total[:, 2 * head_dim :].T
        gain_o[...] = lines[:4]
        head_o[...] = lines[4:6, :head_rows]

    kv_sum = kv_mine_sum
    bit = n_tp // 2
    while bit > 1:
        pair = (kv_sum, swap(kv_sum, "tp", n_tp, bit))
        (kv_sum,) = kernel_call(pair_body, pair, [(kv_sum.shape, bf16)])
        bit //= 2
    kv_grad, gain_grad, head_gain_grad = kernel_call(
        kv_body,
        (kv_sum, swap(kv_sum, "tp", n_tp, bit)),
        [((out_rows, 2 * head_dim), f32), ((4, out_rows), f32), ((2, head_rows), f32)],
    )

    def input_back_body(hid, gains, *refs):
        d_mix = joined(refs[:streams])
        d_normed = summed(refs[streams:-1])
        x = hid[own_rows(0), :].astype(f32)
        scale = rms_scale(x)
        refs[-1][...] = (d_mix + rms_back(d_normed, x * scale, scale, gains[0:1, :])).astype(bf16)

    (input_mine,) = kernel_call(input_back_body, (hidden, norm_gains, *d_mixed, *dn_terms), [((share, width), bf16)])

    def place_body(a, b, o):
        o[own_rows(0), :] = a[...]
        o[own_rows(1), :] = b[...]

    def placed(mine, near):
        (whole,) = kernel_call(place_body, (mine, near), [((rows, width), bf16)])
        return whole.reshape(hidden_in.shape)

    return (
        placed(hidden_mine, hidden_near),
        placed(input_mine, neighbour(input_mine)),
        query_grad,
        kv_grad,
        out_grad.T,
        gate_grad,
        up_grad,
        down_grad.T,
        gain_grad,
        head_gain_grad,
    )


def solution(mesh):
    return jax.shard_map(
        on_device,
        mesh=mesh,
        in_specs=(
            P("batch", "ctx", None, None),
            P("batch", None),
            P(),
            P(),
            P(),
            P(None, "tp"),
            P(),
            P("tp", None),
            P(None, "tp"),
            P(None, "tp"),
            P("tp", None),
            P("batch", "ctx", None, None),
        ),
        out_specs=(
            P("batch", "ctx", None, None),
            P("batch", "ctx", None, None),
            P(("batch", "ctx"), "tp"),
            P(("batch", "ctx"), None),
            P("tp", ("batch", "ctx")),
            P(("batch", "ctx"), "tp"),
            P(("batch", "ctx"), "tp"),
            P("tp", ("batch", "ctx")),
            P(None, ("batch", "ctx")),
            P(None, ("batch", "ctx")),
        ),
        check_vma=False,
    )
```
